32 devices in a mesh: cell: 8 (over y, x, core), spot: 4 (over z).
Axes of the slice: x: 2, y: 2, z: 4, core: 2. Of those that a mesh axis runs over, the one named last changes fastest.
Arguments:
- logits: float32 [8192, 2048], P('cell', 'spot'), may hold values from -6 to 6
- expression: float32 [8192, 2048], P('cell'), may hold values from 0.1 to 4
- spatial: float32 [2048, 2048], P('spot'), may hold values from 0.1 to 4
- spot_counts: int32 [4], replicated, may hold values from 128 to 1024, as said below
- cell_mask: int32 [8192], P('cell'), may hold values from 0 to 1, as said below
- cell_slide: int32 [8192], P('cell'), may hold values from 0 to 3, as said below
Outputs:
- losses: float32 [4], replicated
- predicted: float32 [2048, 2048], P('spot', 'cell')
- cosines: float32 [4, 2048], P(None, 'cell')
- logit_grad: float32 [8192, 2048], P('cell', 'spot')
- expression_grad: float32 [8192, 2048], P('cell')
The draws below stay inside these ranges and needn't reach their ends.
Inputs may be any that keep to these rules, and one draw needn't show every extreme that they name: `spot_counts`: the counts sum to 2048; the smallest is exactly 128 and the largest exactly 1024. `cell_mask`: cell c < 4 is real and lies on slide c. `cell_slide`: cell c < 4 lies on slide c.
All inputs are finite; a program needn't handle non-finite values.
Results may differ from the reference program's by a relative error of at most 0.0003.
Values sent between devices are 32-bit elements; how exact they have to be, the bound alone decides.
No kernel may reach another device: no remote copies, remote signals or barrier semaphores. Data moves between devices by JAX's collectives and lax.ppermute only.
A program may use at most 128 MiB of HBM per device.

```python
import math
import jax
import jax.numpy as jnp
from jax import lax

GENES = 2048
SLIDES = 4
CELLS = 8192
SPOTS = 2048


def draw_spot_counts(key, part):
    unit_size = SPOTS // 16
    middle_count = SLIDES - 2
    first_key, second_key, third_key = jax.random.split(key, 3)
    spare = 7 - 2 * middle_count
    cut_points = jnp.sort(jax.random.randint(first_key, (middle_count - 1,), 0, spare + 1)).astype(jnp.int32)
    edge_list = jnp.concatenate([jnp.zeros((1,), jnp.int32), cut_points, jnp.full((1,), spare, jnp.int32)])
    middle_units = 2 + edge_list[1:] - edge_list[:-1]
    middle_sizes = middle_units * unit_size
    if middle_count >= 2:
        jitter = jax.random.randint(second_key, (), -(unit_size // 3), unit_size // 3 + 1).astype(jnp.int32)
        middle_sizes = middle_sizes.at[0].add(jitter)
        middle_sizes = middle_sizes.at[1].add(-jitter)
    base = jnp.concatenate([jnp.full((1,), unit_size, jnp.int32), jnp.full((1,), 8 * unit_size, jnp.int32), middle_sizes.astype(jnp.int32)])
    order = jax.random.permutation(third_key, SLIDES)
    return base[order].astype(jnp.int32)


def draw_cell_mask(key, part):
    positions = jnp.arange(CELLS, dtype=jnp.int32)
    drawn = (jax.random.randint(key, (CELLS,), 0, 12) < 11).astype(jnp.int32)
    return jnp.where(positions < SLIDES, 1, drawn).astype(jnp.int32)


def draw_cell_slide(key, part):
    positions = jnp.arange(CELLS, dtype=jnp.int32)
    slide_draw = jax.random.randint(key, (CELLS,), 0, SLIDES)
    return jnp.where(positions < SLIDES, positions, slide_draw).astype(jnp.int32)


def block_scale(own_key, shape, shards, least, high):
    gain, own = 1.0, jax.random.fold_in(own_key, 6)
    for position, shards_of in shards:
        draws = jnp.exp(jax.random.uniform(jax.random.fold_in(own, position), (shards_of,), jnp.float32, least / len(shards), high / len(shards)))
        gain = gain * jnp.repeat(draws, shape[position] // shards_of).reshape([-1 if axis == position else 1 for axis in range(len(shape))])
    return gain


def centred(rng, extent, width, limit, pieces=(), kind=jnp.bfloat16):
    values = width * jax.random.normal(rng, extent, jnp.float32)
    if pieces:
        values = values * block_scale(rng, extent, pieces, -0.22, 0.18)
    return jnp.clip(values, -limit, limit).astype(kind)


def setup_inputs(seed: int = 0) -> dict:
    keys = jax.random.split(jax.random.key(seed), 7)
    logits = centred(keys[0], (CELLS, SPOTS), 1.5, 6.0, ((0, 8), (1, 4)), jnp.float32)
    expression = jnp.clip(jnp.exp(math.log(4.0) - 3.6888794 * jax.random.uniform(keys[1], (CELLS, GENES), jnp.float32) ** block_scale(keys[1], (CELLS, GENES), ((0, 8),), -0.2, 0.2)), 0.1, 4.0)
    spatial = jnp.clip(jnp.exp(math.log(4.0) - 3.6888794 * jax.random.uniform(keys[2], (SPOTS, GENES), jnp.float32) ** block_scale(keys[2], (SPOTS, GENES), ((0, 4),), -0.2, 0.2)), 0.1, 4.0)
    spot_counts = draw_spot_counts(jax.random.fold_in(keys[6], 71), 0)
    cell_mask = draw_cell_mask(jax.random.fold_in(keys[6], 71), 0)
    cell_slide = draw_cell_slide(jax.random.fold_in(keys[6], 71), 0)
    return dict(logits=logits, expression=expression, spatial=spatial, spot_counts=spot_counts, cell_mask=cell_mask, cell_slide=cell_slide)


@jax.custom_vjp
def low(v):
    return lax.optimization_barrier(v.astype(jnp.bfloat16)).astype(jnp.float32)

@jax.custom_vjp
def low_back(v):
    return v

def low_keep(v):
    return (low(v), None)

def low_pass(kept, grad):
    return (grad,)

def back_keep(v):
    return (v, None)

def back_low(kept, grad):
    return (low(grad),)
low.defvjp(low_keep, low_pass)
low_back.defvjp(back_keep, back_low)
NEG = -1e+30

def reference(logits, expression, spatial, spot_counts, cell_mask, cell_slide):
    slide_ends = jnp.cumsum(spot_counts).astype(jnp.int32)
    spot_ids = jnp.arange(SPOTS, dtype=jnp.int32)
    spot_slide = lax.optimization_barrier(jnp.sum((spot_ids[:, None] >= slide_ends[None, :SLIDES - 1]).astype(jnp.int32), axis=1))
    member = (cell_mask[:, None] == 1) & (cell_slide[:, None] == spot_slide[None, :])
    spot_onehot = (spot_slide[:, None] == jnp.arange(SLIDES, dtype=jnp.int32)[None, :]).astype(jnp.float32)
    high = lax.Precision.HIGHEST

    def forward(logit_in, expr_in):
        masked = jnp.where(member, logit_in, NEG)
        column_max = lax.optimization_barrier(jnp.max(masked, axis=0))
        exponent = jnp.exp(masked - column_max[None, :])
        mapping = exponent / lax.optimization_barrier(jnp.sum(exponent, axis=0))[None, :]
        predicted = lax.dot_general(mapping, expr_in, (((0,), (0,)), ((), ())), precision=high)
        sum_a = jnp.dot(spot_onehot.T, predicted * spatial, precision=high)
        sum_b = jnp.dot(spot_onehot.T, predicted * predicted, precision=high)
        sum_c = jnp.dot(spot_onehot.T, spatial * spatial, precision=high)
        cosines = sum_a * lax.rsqrt(sum_b) * lax.rsqrt(sum_c)
        losses = -lax.optimization_barrier(jnp.sum(cosines, axis=1))
        return (jnp.sum(losses), (losses, predicted, cosines))
    loss_sum, pullback, extras = jax.vjp(forward, logits, expression, has_aux=True)
    logit_grad, expression_grad = pullback(jnp.ones_like(loss_sum))
    losses, predicted, cosines = extras
    return (losses, predicted, cosines, logit_grad, expression_grad)
```

```python
import functools

import jax
import jax.numpy as jnp
from jax import lax
from jax.experimental import pallas as pl
from jax.experimental.pallas import tpu as pltpu
from jax.sharding import PartitionSpec as P

HIGH = lax.Precision.HIGHEST
F32, BF16, I32 = jnp.float32, jnp.bfloat16, jnp.int32
CAPACITY = 320
EXTRA = 8


def split(x):
    hi = x.astype(BF16)
    return hi, (x - hi.astype(F32)).astype(BF16)


def mm(a, b, dims=((1,), (0,))):
    return lax.dot_general(a, b, (dims, ((), ())), preferred_element_type=F32)


def mm3(ah, al, bh, bl, dims=((1,), (0,))):
    return mm(ah, bh, dims) + (mm(ah, bl, dims) + mm(al, bh, dims))


def slide_of(ids, sc):
    return sum((ids >= sc[k]).astype(I32) for k in range(3))


def prep_kernel(sc, logits, code, e_out, eth_out, etl_out, compact_out, extra_out, rank_out, rbuf, hbuf, lbuf):
    cells, spots = logits.shape
    cap = compact_out.shape[0]
    step = 128
    lane = lax.broadcasted_iota(I32, (1, spots), 1) + sc[4]
    spot_slide = slide_of(lane, sc)
    lanes = lax.broadcasted_iota(I32, (1, step), 1)
    lower = (
        lax.broadcasted_iota(I32, (step, step), 0) > lax.broadcasted_iota(I32, (step, step), 1)
    ).astype(BF16)

    def body(t, carry):
        total, seen = carry
        rows = pl.ds(pl.multiple_of(t * step, step), step)
        own = code[rows, :]
        e = jnp.where(own == spot_slide, jnp.exp(logits[rows, :]), 0.0)
        e_out[rows, :] = e
        hi, lo = split(e)
        hbuf[rows, :] = hi
        lbuf[rows, :] = lo
        hit, lit = split(e.T)
        eth_out[:, rows] = hit
        etl_out[:, rows] = lit
        onehot = (own == lanes).astype(F32)
        before = mm(lower, onehot.astype(BF16)) + seen
        rank = jnp.sum(onehot * before, axis=1, keepdims=True)
        rank = jnp.where(own >= 0, rank, -1.0)
        rank_out[rows, :] = rank.astype(I32)
        row = jnp.broadcast_to(rank, (step, step)).T[:1, :].astype(I32)
        rbuf[:, rows] = (lax.broadcasted_iota(I32, (cap, step), 0) == row).astype(F32).astype(BF16)
        return total + jnp.sum(e, axis=0, keepdims=True), seen + jnp.sum(onehot, axis=0, keepdims=True)

    total, seen = lax.fori_loop(
        0, cells // step, body, (jnp.zeros((1, spots), F32), jnp.zeros((1, step), F32))
    )
    compact_out[...] = mm(rbuf[...], hbuf[...]) + mm(rbuf[...], lbuf[...])
    width = extra_out.shape[1]
    extra_out[...] = jnp.zeros_like(extra_out)
    for h in range(spots // width):
        extra_out[h : h + 1, :] = total[:, h * width : (h + 1) * width]
    over = (jnp.max(seen, axis=1, keepdims=True) > cap).astype(F32)
    extra_out[EXTRA - 1 : EXTRA, :] = jnp.broadcast_to(over, (1, width))


def mm1_kernel(sc, eth, etl, expr, extra, out):
    xh, xl = split(expr[...])
    spots = eth.shape[0]
    out[0, :spots, :] = mm3(eth[...], etl[...], xh, xl)
    out[0, spots:, :] = extra[...]


def totals(extra_rows, spots):
    width = extra_rows.shape[1]
    cols = [
        jnp.broadcast_to(extra_rows[h : h + 1, :], (128, width)).T[:, :1] for h in range(spots // width)
    ]
    return jnp.concatenate(cols, axis=0)


def sums_kernel(sc, a1, a2, b1, b2, spatial, pred_out, sums_out, extra_out):
    spots = pred_out.shape[0]
    half = a1.shape[0]
    low = b1[...] + b2[...]
    extra = low[spots - half :, :]
    extra_out[...] = extra
    z = totals(extra, spots)
    raw = jnp.concatenate([a1[...] + a2[...], low[: spots - half, :]], axis=0)
    pred = raw / z
    pred_out[...] = pred
    spat = spatial[...]
    ids = lax.broadcasted_iota(I32, (spots, 1), 0) + sc[4]
    slide = slide_of(ids, sc)
    sums_out[...] = jnp.zeros_like(sums_out)
    for n, term in enumerate((pred * spat, pred * pred, spat * spat)):
        for k in range(4):
            sums_out[4 * n + k : 4 * n + k + 1, :] = jnp.sum(
                jnp.where(slide == k, term, 0.0), axis=0, keepdims=True
            )


def grad_kernel(parts, sc, pred, spatial, extra, *refs):
    sums, (blk_out, cos_out) = refs[:parts], refs[parts:]
    spots, width = pred.shape
    level = [r[...] for r in sums]
    while len(level) > 1:
        level = [level[n] + level[n + 1] for n in range(0, len(level), 2)]
    a, b, c = level[0][0:4, :], level[0][4:8, :], level[0][8:12, :]
    inv = lax.rsqrt(b) * lax.rsqrt(c)
    cos = a * inv
    ratio = cos / b
    cos_out[...] = cos
    ids = lax.broadcasted_iota(I32, (spots, 1), 0) + sc[4]
    slide = slide_of(ids, sc)
    spread_inv, spread_cos = inv[3:4, :], ratio[3:4, :]
    for k in range(3):
        spread_inv = jnp.where(slide == k, inv[k : k + 1, :], spread_inv)
        spread_cos = jnp.where(slide == k, ratio[k : k + 1, :], spread_cos)
    p = pred[...]
    grad = -(spatial[...] * spread_inv - p * spread_cos) / totals(extra[...], spots)
    blk_out[:spots, :] = grad
    dots = lax.dot_general(
        jnp.ones((8, width), F32), p * grad, (((1,), (1,)), ((), ())),
        precision=HIGH, preferred_element_type=F32,
    )
    blk_out[spots:, :] = jnp.zeros((EXTRA, width), F32)
    for h in range(spots // width):
        blk_out[spots + h : spots + h + 1, :] = dots[:1, h * width : (h + 1) * width]
    blk_out[spots + 4 : spots + 8, :] = cos


def logit_kernel(steps, sc, expr, mine, sib, e, out, acc, dots):
    q = pl.program_id(0)
    cells, spots = e.shape
    width = mine.shape[2]

    @pl.when(q == 0)
    def _():
        acc[...] = jnp.zeros_like(acc)
        dots[...] = jnp.zeros_like(dots)

    parity = lax.rem(sc[3], 2)
    for side, ref in enumerate((mine, sib)):
        start = pl.multiple_of(jnp.where(parity == side, 0, width), width)
        gh, gl = split(ref[0, :spots, :])
        dots[...] += ref[0, spots:, :]

        def body(t, _):
            rows = pl.ds(pl.multiple_of(t * 256, 256), 256)
            xh, xl = split(expr[rows, pl.ds(start, width)])
            acc[rows, :] += mm3(xh, xl, gh, gl, ((1,), (1,)))
            return 0

        lax.fori_loop(0, cells // 256, body, 0, unroll=True)

    @pl.when(q == steps - 1)
    def _():
        row = jnp.concatenate([dots[h : h + 1, :] for h in range(spots // width)], axis=1)
        out[...] = e[...] * (acc[...] - row)


def expr_kernel(kinds, has_acc, sc, *refs):
    refs = list(refs)
    code, rank = refs.pop(0), refs.pop(0)
    layers = [(kind, refs.pop(0), refs.pop(0), refs.pop(0)) for kind in kinds]
    acc = refs.pop(0) if has_acc else None
    out, hbuf, lbuf = refs
    _, cells, spots = hbuf.shape
    q = pl.program_id(0)

    @pl.when(q == 0)
    def _():
        for n, (kind, src, _, _) in enumerate(layers):
            if kind:
                ch, cl = split(src[...])
                cap = src.shape[0]
                lane = lax.broadcasted_iota(I32, (1, spots), 1) + sc[4 + kind]
                spot_slide = slide_of(lane, sc)
                slots = lax.broadcasted_iota(I32, (1, cap), 1)

            def body(t, _):
                rows = pl.ds(pl.multiple_of(t * 256, 256), 256)
                if kind:
                    pick = (rank[rows, :] == slots).astype(F32).astype(BF16)
                    member = code[rows, :] == spot_slide
                    hbuf[n, rows, :] = jnp.where(member, mm(pick, ch), 0.0).astype(BF16)
                    lbuf[n, rows, :] = jnp.where(member, mm(pick, cl), 0.0).astype(BF16)
                else:
                    hi, lo = split(src[rows, :])
                    hbuf[n, rows, :] = hi
                    lbuf[n, rows, :] = lo
                return 0

            lax.fori_loop(0, cells // 256, body, 0)

    width = layers[0][2].shape[2]
    parity = lax.rem(sc[3], 2)
    for side in range(2):
        start = pl.multiple_of(jnp.where(parity == side, 0, width), width)
        grads = [split(layer[2 + side][0, :spots, :]) for layer in layers]

        def body(t, _):
            rows = pl.ds(pl.multiple_of(t * 256, 256), 256)
            value = None
            for n, (gh, gl) in enumerate(grads):
                term = mm3(hbuf[n, rows, :], lbuf[n, rows, :], gh, gl)
                value = term if value is None else value + term
            if acc is not None:
                value = acc[rows, pl.ds(start, width)] + value
            out[rows, pl.ds(start, width)] = value
            return 0

        lax.fori_loop(0, cells // 256, body, 0, unroll=True)


def whole(shape):
    return pl.BlockSpec(shape, lambda *_: (0,) * len(shape))


def call(kernel, sc, args, in_specs, outs, out_specs, grid=(1,), scratch=(), flops=0, name=None):
    size = sum(a.size * a.dtype.itemsize for a in args)
    size += sum(o.size * o.dtype.itemsize for o in jax.tree.leaves(outs))
    return pl.pallas_call(
        kernel,
        out_shape=outs,
        grid_spec=pltpu.PrefetchScalarGridSpec(
            num_scalar_prefetch=1, grid=grid, in_specs=in_specs, out_specs=out_specs, scratch_shapes=scratch
        ),
        cost_estimate=pl.CostEstimate(flops=flops, bytes_accessed=size, transcendentals=0),
        name=name,
    )(sc, *args)


def fast(logits, expression, spatial, spot_counts, cell_mask, cell_slide):
    cells, spots = logits.shape
    genes = expression.shape[1]
    n_cell, n_spot = lax.axis_size("cell"), lax.axis_size("spot")
    width = genes // n_cell
    quads = n_cell // 2
    ci, zi = lax.axis_index("cell"), lax.axis_index("spot")
    ends = jnp.cumsum(spot_counts).astype(I32)
    bases = [(zi ^ k) * spots for k in range(n_spot)]
    sc = jnp.concatenate([ends[:3], jnp.stack([ci, *bases]).astype(I32)])
    code = jnp.where(cell_mask == 1, cell_slide, -1).astype(I32)[:, None]
    sds = jax.ShapeDtypeStruct
    smem_scratch = [
        pltpu.VMEM((CAPACITY, cells), BF16),
        pltpu.VMEM((cells, spots), BF16),
        pltpu.VMEM((cells, spots), BF16),
    ]

    def cell_swap(x, bit):
        return lax.ppermute(x, "cell", [(i, i ^ bit) for i in range(n_cell)])

    def spot_swap(x, k):
        return lax.ppermute(x, "spot", [(i, i ^ k) for i in range(n_spot)])

    e, eth, etl, compact, extra, rank = call(
        prep_kernel, sc, (logits, code),
        [whole((cells, spots)), whole((cells, 1))],
        (
            sds((cells, spots), F32), sds((spots, cells), BF16), sds((spots, cells), BF16),
            sds((CAPACITY, spots), F32), sds((EXTRA, width), F32), sds((cells, 1), I32),
        ),
        (
            whole((cells, spots)), whole((spots, cells)), whole((spots, cells)),
            whole((CAPACITY, spots)), whole((EXTRA, width)), whole((cells, 1)),
        ),
        scratch=smem_scratch, flops=4 * cells * spots * CAPACITY, name="prep",
    )
    compacts = {k: spot_swap(compact, k) for k in range(1, n_spot)}

    rows = spots + EXTRA

    def partial(odd):
        return call(
            mm1_kernel, sc, (eth, etl, expression, extra),
            [
                whole((spots, cells)), whole((spots, cells)),
                pl.BlockSpec((cells, width), lambda g, sc: (0, sc[3] ^ (2 * g + odd))),
                whole((EXTRA, width)),
            ],
            sds((quads, rows, width), F32),
            pl.BlockSpec((1, rows, width), lambda g, sc: (g, 0, 0)),
            grid=(quads,), flops=6 * cells * spots * width * quads, name="mm1",
        )

    odd = partial(1)
    odd_in = cell_swap(odd, 1)
    even = partial(0)
    half = spots // 2
    kept = {(q, s): even[q, sl] + odd_in[q, sl] for q in range(4) for s, sl in ((0, slice(0, half)), (1, slice(half, rows)))}
    send_a = jnp.stack([kept[1, 0], kept[3, 0]])
    send_b = jnp.stack([kept[2, 1], kept[3, 1]])
    in_a = cell_swap(send_a, 2)
    in_b = cell_swap(send_b, 4)
    in_a2 = cell_swap(kept[2, 0] + in_a[1], 4)
    in_b2 = cell_swap(kept[1, 1] + in_b[1], 2)
    own_spatial = pl.BlockSpec((spots, width), lambda g, sc: (0, sc[3]))
    predicted, sums, extra_all = call(
        sums_kernel, sc, (kept[0, 0] + in_a[0], in_a2, kept[0, 1] + in_b[0], in_b2, spatial),
        [whole((half, width)), whole((half, width)), whole((rows - half, width)), whole((rows - half, width)), own_spatial],
        (sds((spots, width), F32), sds((16, width), F32), sds((EXTRA, width), F32)),
        (whole((spots, width)), whole((16, width)), whole((EXTRA, width))),
        name="sums",
    )
    all_sums = [sums, *(spot_swap(sums, k) for k in range(1, n_spot))]
    block, cosines = call(
        functools.partial(grad_kernel, n_spot), sc, (predicted, spatial, extra_all, *all_sums),
        [whole((spots, width)), own_spatial, whole((EXTRA, width)), *[whole((16, width))] * n_spot],
        (sds((rows, width), F32), sds((4, width), F32)),
        (whole((rows, width)), whole((4, width))),
        name="grad",
    )

    def gather(blk):
        a, b = blk[:half], blk[half:]
        ax, by = cell_swap(a, 2), cell_swap(b, 4)
        a2, b2 = jnp.stack([a, ax]), jnp.stack([b, by])
        ay, bx = cell_swap(a2, 4), cell_swap(b2, 2)
        mine = jnp.concatenate(
            [jnp.stack([a, ax, ay[0], ay[1]]), jnp.stack([b, bx[0], by, bx[1]])], axis=1
        )
        return mine, cell_swap(mine, 1)

    remote = {k: spot_swap(block[:spots], k) for k in range(1, n_spot)}
    mine, sib = gather(block)

    pair = lambda sc, q: (sc[3] // 2) ^ q
    logit_grad = call(
        functools.partial(logit_kernel, quads), sc, (expression, mine, sib, e),
        [
            pl.BlockSpec((cells, 2 * width), lambda q, sc: (0, pair(sc, q))),
            pl.BlockSpec((1, rows, width), lambda q, sc: (q, 0, 0)),
            pl.BlockSpec((1, rows, width), lambda q, sc: (q, 0, 0)),
            whole((cells, spots)),
        ],
        sds((cells, spots), F32), whole((cells, spots)), grid=(quads,),
        scratch=[pltpu.VMEM((cells, spots), F32), pltpu.VMEM((EXTRA, width), F32)],
        flops=6 * cells * spots * genes, name="logit",
    )

    def expr_part(layers, acc):
        args, specs = [code, rank], [whole((cells, 1)), whole((cells, 1))]
        for kind, src, m, s in layers:
            args += [src, m, s]
            specs += [whole(src.shape)] + [pl.BlockSpec((1, x.shape[1], width), lambda q, sc: (q, 0, 0)) for x in (m, s)]
        block_spec = pl.BlockSpec((cells, 2 * width), lambda q, sc: (0, pair(sc, q)))
        if acc is not None:
            args.append(acc)
            specs.append(block_spec)
        return call(
            functools.partial(expr_kernel, [layer[0] for layer in layers], acc is not None), sc, args, specs,
            sds((cells, genes), F32), block_spec, grid=(quads,),
            scratch=[pltpu.VMEM((len(layers), cells, spots), BF16)] * 2,
            flops=6 * cells * spots * genes * len(layers), name="expr",
        )

    own = (0, e, mine, sib)
    far = {k: (k, compacts[k], *gather(remote[k])) for k in range(1, n_spot)}
    near = expr_part([own, far[1]], None)

    def direct(operands):
        near, own, far2, far3 = operands
        return expr_part([(2, *far2), (3, *far3)], near)

    def exchange(operands):
        near, own, far2, far3 = operands
        term = expr_part([(0, *own)], None)
        one, two, three = (spot_swap(term, k) for k in (1, 2, 3))
        return (term + one) + (two + three)

    expression_grad = lax.cond(
        extra_all[EXTRA - 1, 0] > 0, exchange, direct, (near, own[1:], far[2][1:], far[3][1:])
    )

    order = jnp.arange(n_cell, dtype=I32) ^ ci
    every = jnp.stack([mine[:, spots + 4 :, :], sib[:, spots + 4 :, :]], axis=1).reshape(n_cell, 4, width)
    losses = -jnp.sum(jnp.take(jnp.sum(every, axis=2), order, axis=0), axis=0)
    return losses, predicted, cosines, logit_grad, expression_grad


def plain(logits, expression, spatial, spot_counts, cell_mask, cell_slide):
    spot_cols = logits.shape[1]
    gene_total = expression.shape[1]
    slide_total = spot_counts.shape[0]
    gene_rows = gene_total // lax.axis_size("cell")
    gene_start = lax.axis_index("cell") * gene_rows
    slide_ends = jnp.cumsum(spot_counts)
    spot_ids = lax.axis_index("spot") * spot_cols + jnp.arange(spot_cols, dtype=I32)
    spot_slide = jnp.sum((spot_ids[:, None] >= slide_ends[None, : slide_total - 1]).astype(I32), axis=1)
    member = (cell_mask[:, None] == 1) & (cell_slide[:, None] == spot_slide[None, :])
    onehot = (spot_slide[:, None] == jnp.arange(slide_total, dtype=I32)[None, :]).astype(F32)
    exponent = jnp.where(member, jnp.exp(logits), 0.0)
    column_total = lax.psum(jnp.sum(exponent, axis=0), "cell")
    mapping = exponent / column_total[None, :]
    predicted = lax.psum_scatter(
        lax.dot_general(expression, mapping, (((0,), (0,)), ((), ())), precision=HIGH),
        "cell", scatter_dimension=0, tiled=True,
    ).T
    spatial_own = lax.dynamic_slice_in_dim(spatial, gene_start, gene_rows, 1)
    sum_a, sum_b, sum_c = lax.psum(
        tuple(
            jnp.dot(onehot.T, t, precision=HIGH)
            for t in (predicted * spatial_own, predicted * predicted, spatial_own * spatial_own)
        ),
        "spot",
    )
    inverse_norms = lax.rsqrt(sum_b) * lax.rsqrt(sum_c)
    cosines = sum_a * inverse_norms
    spread_inv = jnp.dot(onehot, inverse_norms, precision=HIGH)
    spread_cos = jnp.dot(onehot, cosines / sum_b, precision=HIGH)
    pred_grad = -(spatial_own * spread_inv - predicted * spread_cos)
    losses, column_dot = lax.psum((-jnp.sum(cosines, axis=1), jnp.sum(predicted * pred_grad, axis=1)), "cell")
    grad_full = lax.all_gather(pred_grad, "cell", axis=1, tiled=True)
    map_grad = lax.dot_general(expression, grad_full, (((1,), (1,)), ((), ())), precision=HIGH)
    logit_grad = mapping * (map_grad - column_dot[None, :])
    expression_grad = lax.psum(jnp.dot(mapping, grad_full, precision=HIGH), "spot")
    return losses, predicted, cosines, logit_grad, expression_grad


def solution(mesh):
    small = mesh.shape["cell"] == 8 and mesh.shape["spot"] == 4
    return jax.shard_map(
        fast if small else plain,
        mesh=mesh,
        in_specs=(P("cell", "spot"), P("cell", None), P("spot", None), P(), P("cell"), P("cell")),
        out_specs=(P(), P("spot", "cell"), P(None, "cell"), P("cell", "spot"), P("cell", None)),
        check_vma=False,
    )
```

```python
import functools

import jax
import jax.numpy as jnp
from jax import lax
from jax.experimental import pallas as pl
from jax.experimental.pallas import tpu as pltpu
from jax.sharding import PartitionSpec as P

HIGH = lax.Precision.HIGHEST
F32, BF16, I32 = jnp.float32, jnp.bfloat16, jnp.int32
CAPACITY = 304
EXTRA = 8
WINDOW = 64
MIDDLE = ((1, 2), (2, 1))
OUTWARD = ((1, 0), (2, 3))
COUNTS, CELL, BASE, ORDER = 0, 4, 5, 9
BLOCKS = (7, 6, 3, 5, 1, 2, 4, 0)


def split(x):
    hi = x.astype(BF16)
    return hi, (x - hi.astype(F32)).astype(BF16)


def mm(a, b, dims=((1,), (0,))):
    return lax.dot_general(a, b, (dims, ((), ())), preferred_element_type=F32)


def mm3(ah, al, bh, bl, dims=((1,), (0,))):
    return mm(ah, bh, dims) + (mm(ah, bl, dims) + mm(al, bh, dims))


def slide_of(ids, sc):
    end, slide = 0, 0
    for k in range(3):
        end = end + sc[COUNTS + k]
        slide = slide + (ids >= end).astype(I32)
    return slide


def block_rows(t, step):
    return pl.ds(pl.multiple_of(t * step, step), step)


def first_kernel(sc, logits, mask, slide, expr, *refs):
    hi_out, lo_out, eth, etl, compact_out, extra_out, place_out, table_out, *refs = refs
    *outs, rbuf, obuf, sem = refs
    cells, spots = logits.shape
    cap, width = compact_out.shape[0], extra_out.shape[1]
    step = 128
    g = pl.program_id(0)

    @pl.when(g == 0)
    def _():
        lane = lax.broadcasted_iota(I32, (1, spots), 1) + sc[BASE]
        spot_slide = slide_of(lane, sc)
        lanes = lax.broadcasted_iota(I32, (1, step), 1).astype(F32)
        lower = (
            lax.broadcasted_iota(I32, (step, step), 0) > lax.broadcasted_iota(I32, (step, step), 1)
        ).astype(BF16)

        def body(t, carry):
            total, seen, widest = carry
            rows = block_rows(t, step)
            one = pl.ds(t, 1)
            own_row = jnp.where(mask[one, :] == 1, slide[one, :], -1).astype(F32)
            own = jnp.broadcast_to(own_row, (step, step)).T[:, :1]
            e = jnp.where(own.astype(I32) == spot_slide, jnp.exp(logits[rows, :]), 0.0)
            hi, lo = split(e)
            e = hi.astype(F32) + lo.astype(F32)
            hi, lo = split(e)
            hi_out[rows, :] = hi
            lo_out[rows, :] = lo
            hit, lit = split(e.T)
            eth[:, rows] = hit
            etl[:, rows] = lit
            onehot = (own == lanes).astype(F32)
            before = mm(lower, onehot.astype(BF16)) + seen
            rank = jnp.sum(onehot * before, axis=1, keepdims=True)
            rank = jnp.where(own >= 0, rank, -1.0)
            window = jnp.minimum((seen.astype(I32) // 8) * 8, cap - WINDOW)
            table_out[one, :] = window
            window = window.astype(F32)
            local = jnp.sum(onehot * (before - window), axis=1, keepdims=True) + WINDOW * own
            place_out[rows, :] = jnp.where(own >= 0, local, -1.0).astype(I32)
            row = jnp.broadcast_to(rank, (step, step)).T[:1, :].astype(I32)
            rbuf[:, rows] = (lax.broadcasted_iota(I32, (cap, step), 0) == row).astype(F32).astype(BF16)
            after = seen + jnp.sum(onehot, axis=0, keepdims=True)
            return total + jnp.sum(e, axis=0, keepdims=True), after, jnp.maximum(widest, after - window)

        zero = jnp.zeros((1, step), F32)
        total, seen, widest = lax.fori_loop(
            0, cells // step, body, (jnp.zeros((1, spots), F32), zero, zero)
        )
        compact_out[...] = mm(rbuf[...], hi_out[...]) + mm(rbuf[...], lo_out[...])
        extra_out[...] = jnp.zeros_like(extra_out)
        for h in range(spots // width):
            extra_out[h : h + 1, :] = total[:, h * width : (h + 1) * width]
        over = jnp.maximum((seen > cap).astype(F32), (widest > WINDOW).astype(F32))
        over = jnp.max(over, axis=1, keepdims=True)
        extra_out[EXTRA - 1 : EXTRA, :] = jnp.broadcast_to(over, (1, width))

    product(g, eth, etl, expr, extra_out, outs, obuf, sem)


def product(g, eth, etl, expr, extra, outs, obuf, sem):
    spots = eth.shape[0]
    count = len(outs)
    slot = lax.rem(g, 2)

    def put(n):
        return pltpu.make_async_copy(obuf.at[n % 2], outs[n], sem.at[n % 2])

    for n in range(2, count):

        @pl.when(g == n)
        def _():
            put(n - 2).wait()

    xh, xl = split(expr[...])
    obuf[slot, :spots, :] = mm3(eth[...], etl[...], xh, xl)
    obuf[slot, spots:, :] = extra[...]
    for n in range(count):

        @pl.when(g == n)
        def _():
            put(n).start()

    @pl.when(g == count - 1)
    def _():
        for n in range(count - 2, count):
            put(n).wait()


def more_kernel(sc, eth, etl, expr, extra, *refs):
    *outs, obuf, sem = refs
    views = [out.at[n] for out in outs for n in range(out.shape[0])]
    product(pl.program_id(0), eth, etl, expr, extra, views, obuf, sem)


def diagonal_kernel(sc, a, b, top, bottom):
    half = top.shape[0]
    top[...] = a[:half, :] + b[:half, :]
    bottom[...] = a[half:, :] + b[half:, :]


def merge_kernel(sc, a, b, low, high, one, two):
    half = high.shape[0]
    one[:half, :] = a[0, :half, :] + b[0, :half, :]
    one[half:, :] = (a[0, half:, :] + b[0, half:, :]) + low[...]
    two[:half, :] = (a[1, :half, :] + b[1, :half, :]) + high[...]
    two[half:, :] = a[1, half:, :] + b[1, half:, :]


def totals(extra_rows, spots):
    width = extra_rows.shape[1]
    cols = [
        jnp.broadcast_to(extra_rows[h : h + 1, :], (128, width)).T[:, :1] for h in range(spots // width)
    ]
    return jnp.concatenate(cols, axis=0)


def sums_kernel(sc, a, b, x, y, spatial, pred_out, sums_out, extra_out):
    spots = pred_out.shape[0]
    extra = (a[spots:, :] + b[spots:, :]) + (x[spots:, :] + y[spots:, :])
    extra_out[...] = extra
    z = totals(extra, spots)
    pred = ((a[:spots, :] + b[:spots, :]) + (x[:spots, :] + y[:spots, :])) / z
    pred_out[...] = pred
    spat = spatial[...]
    ids = lax.broadcasted_iota(I32, (spots, 1), 0) + sc[BASE]
    slide = slide_of(ids, sc)
    sums_out[...] = jnp.zeros_like(sums_out)
    for n, term in enumerate((pred * spat, pred * pred, spat * spat)):
        for k in range(4):
            sums_out[4 * n + k : 4 * n + k + 1, :] = jnp.sum(
                jnp.where(slide == k, term, 0.0), axis=0, keepdims=True
            )


def grad_kernel(sc, pred, spatial, extra, s0, s1, s2, s3, blk_out, cos_out):
    spots, width = pred.shape
    sums = (s0[...] + s1[...]) + (s2[...] + s3[...])
    a, b, c = sums[0:4, :], sums[4:8, :], sums[8:12, :]
    inv = lax.rsqrt(b) * lax.rsqrt(c)
    cos = a * inv
    ratio = cos / b
    cos_out[...] = cos
    ids = lax.broadcasted_iota(I32, (spots, 1), 0) + sc[BASE]
    slide = slide_of(ids, sc)
    spread_inv, spread_cos = inv[3:4, :], ratio[3:4, :]
    for k in range(3):
        spread_inv = jnp.where(slide == k, inv[k : k + 1, :], spread_inv)
        spread_cos = jnp.where(slide == k, ratio[k : k + 1, :], spread_cos)
    p = pred[...]
    grad = -(spatial[...] * spread_inv - p * spread_cos) / totals(extra[...], spots)
    blk_out[:spots, :] = grad
    dots = lax.dot_general(
        jnp.ones((8, width), F32), p * grad, (((1,), (1,)), ((), ())),
        precision=HIGH, preferred_element_type=F32,
    )
    blk_out[spots:, :] = jnp.zeros((EXTRA, width), F32)
    for h in range(spots // width):
        blk_out[spots + h : spots + h + 1, :] = dots[:1, h * width : (h + 1) * width]
    blk_out[spots + 4 : spots + 8, :] = cos


def fetch(g, steps, blocks, buf, sem):
    per = len(blocks) // steps

    def copies(s):
        return [pltpu.make_async_copy(blocks[s * per + n], buf.at[s, n], sem.at[s, n]) for n in range(per)]

    @pl.when(g == 0)
    def _():
        for s in range(steps):
            for c in copies(s):
                c.start()

    for s in range(steps):

        @pl.when(g == s)
        def _():
            for c in copies(s):
                c.wait()

    return buf.at[g]


def logit_kernel(steps, sc, expr, *refs):
    blocks, (hi, lo, out, loss_out, acc, dots, parts, buf, sem) = refs[: 2 * steps], refs[2 * steps :]
    g = pl.program_id(0)
    cells, spots = acc.shape
    width = buf.shape[3]
    got = fetch(g, steps, blocks, buf, sem)

    @pl.when(g == 0)
    def _():
        acc[...] = jnp.zeros_like(acc)
        dots[...] = jnp.zeros_like(dots)

    parity = lax.rem(sc[CELL], 2)
    for side in range(2):
        start = pl.multiple_of(jnp.where(parity == side, 0, width), width)
        gh, gl = split(got[side, :spots, :])
        dots[...] += got[side, spots:, :]
        sums = jnp.sum(got[side, spots:, :], axis=1, keepdims=True)
        parts[sc[CELL] ^ (2 * g + side)] = jnp.broadcast_to(sums, parts.shape[1:])

        def body(t, _):
            rows = block_rows(t, 256)
            xh, xl = split(expr[rows, pl.ds(start, width)])
            acc[rows, :] += mm3(xh, xl, gh, gl, ((1,), (1,)))
            return 0

        lax.fori_loop(0, cells // 256, body, 0, unroll=True)

    @pl.when(g == steps - 1)
    def _():
        row = jnp.concatenate([dots[h : h + 1, :] for h in range(spots // width)], axis=1)
        e = hi[...].astype(F32) + lo[...].astype(F32)
        out[...] = e * (acc[...] - row)
        total = parts[0]
        for n in range(1, parts.shape[0]):
            total = total + parts[n]
        loss_out[...] = -total


def rows_kernel(steps, alias, sc, table, *refs):
    blocks, refs = refs[: 8 * steps], refs[8 * steps :]
    comps, place, refs = refs[:4], refs[4], refs[5 + alias :]
    out, buf, sem, comp, csem, gh, gl, res, sh, sl = refs
    g = pl.program_id(0)
    cells = out.shape[0]
    cap, spots = comp.shape[1:]
    width = buf.shape[3]
    half = spots // 2

    def bring(s, n):
        return pltpu.make_async_copy(blocks[8 * s + n], buf.at[s, n], sem.at[s, n])

    def bring_comp(n):
        return pltpu.make_async_copy(comps[n], comp.at[n], csem.at[n])

    @pl.when(g == 0)
    def _():
        for s in range(steps):
            for layer in range(4):
                if s == 0:
                    bring_comp(layer).start()
                for side in range(2):
                    bring(s, 2 * layer + side).start()

    res[...] = jnp.zeros_like(res)
    parity = lax.rem(sc[CELL], 2)

    def layer_body(layer, _):
        for side in range(2):
            n = 2 * layer + side
            pltpu.make_async_copy(blocks[0], buf.at[g, n], sem.at[g, n]).wait()

        @pl.when(g == 0)
        def _():
            pltpu.make_async_copy(comps[0], comp.at[layer], csem.at[layer]).wait()

        for side in range(2):
            start = pl.multiple_of(jnp.where(parity == side, 0, width), width)
            hi, lo = split(buf[g, 2 * layer + side, :spots, :])
            gh[:, pl.ds(start, width)] = hi
            gl[:, pl.ds(start, width)] = lo
        base = sc[BASE + layer]
        spot_slide = slide_of(lax.broadcasted_iota(I32, (1, spots), 1) + base, sc)
        low, low_end = slide_of(base, sc), slide_of(base + half - 1, sc)
        high, high_end = slide_of(base + half, sc), slide_of(base + spots - 1, sc)
        which = layer // 2

        def slide_body(k, _):
            in_low, in_high = k <= low_end, k >= high

            @pl.when(in_low & in_high)
            def _():
                ch, cl = split(jnp.where(spot_slide == k, comp[layer], 0.0))
                res[which, k] += mm3(ch, cl, gh[...], gl[...])

            @pl.when(jnp.logical_not(in_low & in_high))
            def _():
                first = pl.multiple_of(jnp.where(in_low, 0, half), half)
                part = slide_of(lax.broadcasted_iota(I32, (1, half), 1) + (base + first), sc)
                cols = pl.ds(first, half)
                ch, cl = split(jnp.where(part == k, comp[layer, :, cols], 0.0))
                res[which, k] += mm3(ch, cl, gh[cols, :], gl[cols, :])

            return 0

        lax.fori_loop(low, high_end + 1, slide_body, 0)
        return 0

    lax.fori_loop(0, 4, layer_body, 0)
    slots = lax.broadcasted_iota(I32, (1, 4 * WINDOW), 1)

    def place_body(t, _):
        rows = block_rows(t, 128)
        for k in range(4):
            window = pl.ds(pl.multiple_of(table[t, k], 8), WINDOW)
            hi, lo = split(res[0, k, window, :] + res[1, k, window, :])
            sh[k * WINDOW : (k + 1) * WINDOW, :] = hi
            sl[k * WINDOW : (k + 1) * WINDOW, :] = lo
        pick = (place[rows, :] == slots).astype(F32).astype(BF16)
        out[rows, :] = mm(pick, sh[...]) + mm(pick, sl[...])
        return 0

    lax.fori_loop(0, cells // 128, place_body, 0)


def expr_kernel(steps, layers, near, alias, sc, *refs):
    refs = list(refs)
    blocks = [refs.pop(0) for _ in range(2 * layers * steps)]
    maps = [(refs.pop(0), refs.pop(0)) for _ in range(layers)]
    acc = refs.pop(0) if near else None
    if alias:
        refs.pop(0)
    out, buf, sem = refs
    g = pl.program_id(0)
    cells, spots = maps[0][0].shape
    width = buf.shape[3]
    got = fetch(g, steps, blocks, buf, sem)
    parity = lax.rem(sc[CELL], 2)
    for side in range(2):
        start = pl.multiple_of(jnp.where(parity == side, 0, width), width)
        grads = [split(got[2 * n + side, :spots, :]) for n in range(layers)]

        def body(t, _):
            rows = block_rows(t, 256)
            value = None
            for (mh, ml), (gh, gl) in zip(maps, grads):
                term = mm3(mh[rows, :], ml[rows, :], gh, gl)
                value = term if value is None else value + term
            if acc is not None:
                value = acc[rows, pl.ds(start, width)] + value
            out[rows, pl.ds(start, width)] = value
            return 0

        lax.fori_loop(0, cells // 256, body, 0, unroll=True)


def tie(x, *others):
    return lax.optimization_barrier((x, *others))[0]


def whole(shape):
    return pl.BlockSpec(shape, lambda *_: (0,) * len(shape))


ANY = pl.BlockSpec(memory_space=pl.ANY)


def call(kernel, sc, args, in_specs, outs, out_specs, grid=(1,), scratch=(), flops=0, name=None, alias=None):
    size = sum(a.size * a.dtype.itemsize for a in args)
    size += sum(o.size * o.dtype.itemsize for o in jax.tree.leaves(outs))
    return pl.pallas_call(
        kernel,
        out_shape=outs,
        grid_spec=pltpu.PrefetchScalarGridSpec(
            num_scalar_prefetch=len(sc), grid=grid, in_specs=in_specs, out_specs=out_specs, scratch_shapes=scratch
        ),
        cost_estimate=pl.CostEstimate(flops=flops, bytes_accessed=size, transcendentals=0),
        input_output_aliases=alias or {},
        name=name,
    )(*sc, *args)


def fast(logits, expression, spatial, spot_counts, cell_mask, cell_slide):
    cells, spots = logits.shape
    genes = expression.shape[1]
    n_cell, n_spot = lax.axis_size("cell"), lax.axis_size("spot")
    width = genes // n_cell
    half, rows = spots // 2, spots + EXTRA
    ci, zi = lax.axis_index("cell"), lax.axis_index("spot")
    places = [ci, *((zi ^ k) * spots for k in range(n_spot))]
    sc = (jnp.concatenate([spot_counts, jnp.stack(places), jnp.array(BLOCKS, I32)]).astype(I32),)
    sds = jax.ShapeDtypeStruct
    block_sds, block_spec = sds((rows, width), F32), whole((rows, width))

    put_scratch = [pltpu.VMEM((2, rows, width), F32), pltpu.SemaphoreType.DMA((2,))]

    def cell_swap(x, bit):
        return lax.ppermute(x, "cell", [(i, i ^ bit) for i in range(n_cell)])

    def spot_swap(x, k):
        return lax.ppermute(x, "spot", [(i, i ^ k) for i in range(n_spot)])

    def spot_move(x, moves):
        return lax.ppermute(x, "spot", moves)

    def genes_spec(first):
        return pl.BlockSpec((cells, width), lambda g, sc, *_: (0, sc[CELL] ^ sc[ORDER + first + g]))

    hi, lo, eth, etl, compact, extra, place, table, b7, b6 = call(
        first_kernel, sc, (logits, cell_mask.reshape(-1, 128), cell_slide.reshape(-1, 128), expression),
        [whole((cells, spots)), whole((cells // 128, 128)), whole((cells // 128, 128)), genes_spec(0)],
        (
            sds((cells, spots), BF16), sds((cells, spots), BF16), sds((spots, cells), BF16), sds((spots, cells), BF16),
            sds((CAPACITY, spots), F32), sds((EXTRA, width), F32), sds((cells, 1), I32), sds((cells // 128, 128), I32),
            block_sds, block_sds,
        ),
        (
            whole((cells, spots)), whole((cells, spots)), whole((spots, cells)), whole((spots, cells)),
            whole((CAPACITY, spots)), whole((EXTRA, width)), whole((cells, 1)), whole((cells // 128, 128)), ANY, ANY,
        ),
        grid=(2,), scratch=[pltpu.VMEM((CAPACITY, cells), BF16), *put_scratch],
        flops=4 * cells * spots * CAPACITY + 12 * cells * spots * width, name="first",
    )

    def products(first, parts, extra):
        count = sum(parts)
        return call(
            more_kernel, sc, (eth, etl, expression, extra),
            [whole((spots, cells)), whole((spots, cells)), genes_spec(first), whole((EXTRA, width))],
            tuple(sds((n, rows, width), F32) for n in parts), (ANY,) * len(parts), scratch=put_scratch,
            grid=(count,), flops=6 * cells * spots * width * count, name="more",
        )

    far1, far_m = spot_swap(compact, 1), spot_move(compact, MIDDLE)
    top3, low3 = call(
        diagonal_kernel, sc, (b6, cell_swap(b7, 1)), [block_spec] * 2,
        (sds((half, width), F32), sds((rows - half, width), F32)),
        (whole((half, width)), whole((rows - half, width))), name="diagonal",
    )
    in_top, in_low = cell_swap(top3, 2), cell_swap(low3, 4)
    odd, even = products(2, (3, 3), tie(extra, top3))
    in_odd = cell_swap(tie(odd, in_top, in_low, far1, far_m), 1)
    three_blocks = whole((3, rows, width))
    one, two = call(
        merge_kernel, sc, (even, in_odd, in_low, in_top),
        [three_blocks, three_blocks, whole((rows - half, width)), whole((half, width))],
        (block_sds, block_sds), (block_spec, block_spec), name="merge",
    )
    in_x, in_y = cell_swap(one, 2), cell_swap(two, 4)
    far_n, far_e = spot_move(tie(far1, one), MIDDLE), spot_move(tie(far_m, one), OUTWARD)
    own_spatial = pl.BlockSpec((spots, width), lambda g, sc, *_: (0, sc[CELL]))
    small = whole((16, width))
    one_block = pl.BlockSpec((None, rows, width), lambda *_: (2, 0, 0))
    predicted, sums, extra_all = call(
        sums_kernel, sc, (tie(even, far_n, far_e), in_odd, in_x, in_y, spatial),
        [one_block, one_block, block_spec, block_spec, own_spatial],
        (sds((spots, width), F32), sds((16, width), F32), sds((EXTRA, width), F32)),
        (whole((spots, width)), small, whole((EXTRA, width))), name="sums",
    )
    far_f = spot_move(tie(far_n, in_x, in_y), OUTWARD)
    far2, far3 = far_n + far_e, far_m + far_f
    all_sums = [sums, *(spot_swap(sums, k) for k in range(1, n_spot))]
    block, cosines = call(
        grad_kernel, sc, (tie(predicted, far_f), spatial, extra_all, *all_sums),
        [whole((spots, width)), own_spatial, whole((EXTRA, width))] + [small] * n_spot,
        (block_sds, sds((4, width), F32)), (block_spec, whole((4, width))), name="grad",
    )

    def pair(g, sc, qs):
        q = qs[0]
        for n, value in enumerate(qs):
            q = jnp.where(g == n, value, q) if n else q
        return (sc[CELL] // 2) ^ q

    def logit_part(got):
        blocks = [x for q in range(4) for x in got[q]]
        return call(
            functools.partial(logit_kernel, 4), sc, (expression, *blocks, hi, lo),
            [
                pl.BlockSpec((cells, 2 * width), lambda g, sc, *_: (0, pair(g, sc, (0, 1, 2, 3)))),
                *[ANY] * len(blocks), whole((cells, spots)), whole((cells, spots)),
            ],
            (sds((cells, spots), F32), sds((EXTRA, 128), F32)), (whole((cells, spots)), whole((EXTRA, 128))), grid=(4,),
            scratch=[
                pltpu.VMEM((cells, spots), F32), pltpu.VMEM((EXTRA, width), F32), pltpu.VMEM((n_cell, EXTRA, 128), F32),
                pltpu.VMEM((4, 2, rows, width), F32), pltpu.SemaphoreType.DMA((4, 2)),
            ],
            flops=6 * cells * spots * genes, name="logit",
        )

    def rows_part(gots, comps, qs, onto=None):
        blocks = [x for q in qs for got in gots for x in got[q]]
        args = [*blocks, *comps, place]
        specs = [ANY] * len(blocks) + [ANY] * 4 + [whole((cells, 1))]
        alias = None
        if onto is not None:
            alias = {len(args) + 2: 0}
            args.append(onto)
            specs.append(ANY)
        steps = len(qs)
        return call(
            functools.partial(rows_kernel, steps, int(onto is not None)), (*sc, table), args, specs,
            sds((cells, genes), F32), pl.BlockSpec((cells, 2 * width), lambda g, sc, *_: (0, pair(g, sc, qs))),
            grid=(steps,), alias=alias,
            scratch=[
                pltpu.VMEM((steps, 8, rows, width), F32), pltpu.SemaphoreType.DMA((steps, 8)),
                pltpu.VMEM((4, CAPACITY, spots), F32), pltpu.SemaphoreType.DMA((4,)),
                pltpu.VMEM((spots, 2 * width), BF16), pltpu.VMEM((spots, 2 * width), BF16),
                pltpu.VMEM((2, 4, CAPACITY, 2 * width), F32),
                pltpu.VMEM((4 * WINDOW, 2 * width), BF16), pltpu.VMEM((4 * WINDOW, 2 * width), BF16),
            ],
            flops=6 * CAPACITY * spots * 2 * width * 8 * steps, name="rows",
        )

    def expr_part(gots, maps, qs, near=None, final=False, onto=None):
        blocks = [x for q in qs for got in gots for x in got[q]]
        args = [*blocks, *(m for pairs in maps for m in pairs)]
        specs = [ANY] * len(blocks) + [whole((cells, spots))] * (2 * len(maps))
        columns = pl.BlockSpec((cells, 2 * width), lambda g, sc, *_: (0, pair(g, sc, qs)))
        steps_spec = pl.BlockSpec((None, cells, 2 * width), lambda g, sc, *_: (g, 0, 0))
        alias = None
        if near is not None:
            args.append(near)
            specs.append(steps_spec)
        if onto is not None:
            alias = {len(args) + 1: 0}
            args.append(onto)
            specs.append(ANY)
        out = sds((cells, genes) if final else (len(qs), cells, 2 * width), F32)
        scratch = [
            pltpu.VMEM((len(qs), 2 * len(maps), rows, width), F32),
            pltpu.SemaphoreType.DMA((len(qs), 2 * len(maps))),
        ]
        return call(
            functools.partial(expr_kernel, len(qs), len(maps), near is not None, onto is not None), sc, args, specs,
            out, columns if final else steps_spec, grid=(len(qs),), scratch=scratch, alias=alias,
            flops=6 * cells * spots * 2 * width * len(qs) * len(maps), name="expr",
        )

    def cores(x):
        return (x, cell_swap(x, 1))

    o_x, o_y = cell_swap(block, 2), cell_swap(block, 4)
    z1, mid = spot_swap(block, 1), spot_move(block, MIDDLE)
    got_o = {0: cores(block), 1: cores(o_x), 2: cores(o_y)}
    a_x = cell_swap(tie(z1, o_x), 2)
    o_d = cell_swap(tie(o_x, o_y), 4)
    mid2, end2 = spot_move(tie(z1, mid), MIDDLE), spot_move(tie(mid, z1), OUTWARD)
    z2 = mid2 + end2
    got_o[3] = cores(o_d)
    c_x = cell_swap(tie(z2, a_x), 2)
    a_y = cell_swap(tie(z1, o_d), 4)
    z3 = mid + spot_move(mid2, OUTWARD)
    logit_grad, losses = logit_part(got_o)
    got_a = {0: cores(z1), 1: cores(a_x), 2: cores(a_y)}
    a_d = cell_swap(tie(a_y, c_x, logit_grad), 2)
    c_y = cell_swap(tie(z2, a_y, logit_grad), 4)
    got_c = {0: cores(z2), 1: cores(c_x), 2: cores(c_y)}
    d_x, d_y = cell_swap(tie(z3, a_d), 2), cell_swap(tie(z3, c_y), 4)
    got_a[3] = cores(a_d)
    got_d = {0: cores(z3), 1: cores(d_x), 2: cores(d_y)}
    gots, comps = (got_o, got_a, got_c, got_d), (compact, far1, far2, far3)
    body = rows_part(gots, comps, (0,))
    d_d = cell_swap(tie(d_y, d_x, body), 2)
    c_d = cell_swap(tie(c_x, d_y, body), 4)
    body = rows_part(gots, comps, (1, 2), body)
    got_c[3], got_d[3] = cores(c_d), cores(d_d)

    def direct(operands):
        body, last = operands[:2]
        return rows_part(last, comps, (3,), body)

    def exchange(operands):
        term = expr_part((operands[2],), ((hi, lo),), (0, 1, 2, 3), final=True)
        one, two, three = (spot_swap(term, k) for k in (1, 2, 3))
        return (term + one) + (two + three)

    expression_grad = lax.cond(
        extra_all[EXTRA - 1, 0] > 0, exchange, direct, (body, [{3: got[3]} for got in gots], got_o)
    )

    losses = losses[4:, 0]
    return losses, predicted, cosines, logit_grad, expression_grad


def plain(logits, expression, spatial, spot_counts, cell_mask, cell_slide):
    spot_cols = logits.shape[1]
    gene_total = expression.shape[1]
    slide_total = spot_counts.shape[0]
    gene_rows = gene_total // lax.axis_size("cell")
    gene_start = lax.axis_index("cell") * gene_rows
    slide_ends = jnp.cumsum(spot_counts)
    spot_ids = lax.axis_index("spot") * spot_cols + jnp.arange(spot_cols, dtype=I32)
    spot_slide = jnp.sum((spot_ids[:, None] >= slide_ends[None, : slide_total - 1]).astype(I32), axis=1)
    member = (cell_mask[:, None] == 1) & (cell_slide[:, None] == spot_slide[None, :])
    onehot = (spot_slide[:, None] == jnp.arange(slide_total, dtype=I32)[None, :]).astype(F32)
    exponent = jnp.where(member, jnp.exp(logits), 0.0)
    column_total = lax.psum(jnp.sum(exponent, axis=0), "cell")
    mapping = exponent / column_total[None, :]
    predicted = lax.psum_scatter(
        lax.dot_general(expression, mapping, (((0,), (0,)), ((), ())), precision=HIGH),
        "cell", scatter_dimension=0, tiled=True,
    ).T
    spatial_own = lax.dynamic_slice_in_dim(spatial, gene_start, gene_rows, 1)
    sum_a, sum_b, sum_c = lax.psum(
        tuple(
            jnp.dot(onehot.T, t, precision=HIGH)
            for t in (predicted * spatial_own, predicted * predicted, spatial_own * spatial_own)
        ),
        "spot",
    )
    inverse_norms = lax.rsqrt(sum_b) * lax.rsqrt(sum_c)
    cosines = sum_a * inverse_norms
    spread_inv = jnp.dot(onehot, inverse_norms, precision=HIGH)
    spread_cos = jnp.dot(onehot, cosines / sum_b, precision=HIGH)
    pred_grad = -(spatial_own * spread_inv - predicted * spread_cos)
    losses, column_dot = lax.psum((-jnp.sum(cosines, axis=1), jnp.sum(predicted * pred_grad, axis=1)), "cell")
    grad_full = lax.all_gather(pred_grad, "cell", axis=1, tiled=True)
    map_grad = lax.dot_general(expression, grad_full, (((1,), (1,)), ((), ())), precision=HIGH)
    logit_grad = mapping * (map_grad - column_dot[None, :])
    expression_grad = lax.psum(jnp.dot(mapping, grad_full, precision=HIGH), "spot")
    return losses, predicted, cosines, logit_grad, expression_grad


def solution(mesh):
    small = mesh.shape["cell"] == 8 and mesh.shape["spot"] == 4
    return jax.shard_map(
        fast if small else plain,
        mesh=mesh,
        in_specs=(P("cell", "spot"), P("cell", None), P("spot", None), P(), P("cell"), P("cell")),
        out_specs=(P(), P("spot", "cell"), P(None, "cell"), P("cell", "spot"), P("cell", None)),
        check_vma=False,
    )
```

```python
import functools

import jax
import jax.numpy as jnp
from jax import lax
from jax.experimental import pallas as pl
from jax.experimental.pallas import tpu as pltpu
from jax.sharding import PartitionSpec as P

HIGH = lax.Precision.HIGHEST
F32, BF16, I32 = jnp.float32, jnp.bfloat16, jnp.int32
CAPACITY = 304
EXTRA = 8
WINDOW = 64
MIDDLE = ((1, 2), (2, 1))
OUTWARD = ((1, 0), (2, 3))
COUNTS, CELL, BASE, ORDER = 0, 4, 5, 9
BLOCKS = (7, 6, 3, 5, 1, 2, 4, 0)


def split(x):
    hi = x.astype(BF16)
    return hi, (x - hi.astype(F32)).astype(BF16)


def mm(a, b, dims=((1,), (0,))):
    return lax.dot_general(a, b, (dims, ((), ())), preferred_element_type=F32)


def mm3(ah, al, bh, bl, dims=((1,), (0,))):
    return mm(ah, bh, dims) + (mm(ah, bl, dims) + mm(al, bh, dims))


def slide_of(ids, sc):
    end, slide = 0, 0
    for k in range(3):
        end = end + sc[COUNTS + k]
        slide = slide + (ids >= end).astype(I32)
    return slide


def block_rows(t, step):
    return pl.ds(pl.multiple_of(t * step, step), step)


def first_kernel(sc, logits, mask, slide, expr, *refs):
    hi_out, lo_out, eth, etl, compact_out, extra_out, place_out, table_out, *refs = refs
    *outs, rbuf, obuf, sem = refs
    cells, spots = logits.shape
    cap, width = compact_out.shape[0], extra_out.shape[1]
    step = 128
    g = pl.program_id(0)

    @pl.when(g == 0)
    def _():
        lane = lax.broadcasted_iota(I32, (1, spots), 1) + sc[BASE]
        spot_slide = slide_of(lane, sc)
        lanes = lax.broadcasted_iota(I32, (1, step), 1).astype(F32)
        lower = (
            lax.broadcasted_iota(I32, (step, step), 0) > lax.broadcasted_iota(I32, (step, step), 1)
        ).astype(BF16)

        def body(t, carry):
            total, seen, widest = carry
            rows = block_rows(t, step)
            one = pl.ds(t, 1)
            own_row = jnp.where(mask[one, :] == 1, slide[one, :], -1).astype(F32)
            own = jnp.broadcast_to(own_row, (step, step)).T[:, :1]
            e = jnp.where(own.astype(I32) == spot_slide, jnp.exp(logits[rows, :]), 0.0)
            hi, lo = split(e)
            e = hi.astype(F32) + lo.astype(F32)
            hi, lo = split(e)
            hi_out[rows, :] = hi
            lo_out[rows, :] = lo
            hit, lit = split(e.T)
            eth[:, rows] = hit
            etl[:, rows] = lit
            onehot = (own == lanes).astype(F32)
            before = mm(lower, onehot.astype(BF16)) + seen
            rank = jnp.sum(onehot * before, axis=1, keepdims=True)
            rank = jnp.where(own >= 0, rank, -1.0)
            window = jnp.minimum((seen.astype(I32) // 8) * 8, cap - WINDOW)
            table_out[one, :] = window
            window = window.astype(F32)
            local = jnp.sum(onehot * (before - window), axis=1, keepdims=True) + WINDOW * own
            place_out[rows, :] = jnp.where(own >= 0, local, -1.0).astype(I32)
            row = jnp.broadcast_to(rank, (step, step)).T[:1, :].astype(I32)
            rbuf[:, rows] = (lax.broadcasted_iota(I32, (cap, step), 0) == row).astype(F32).astype(BF16)
            after = seen + jnp.sum(onehot, axis=0, keepdims=True)
            return total + jnp.sum(e, axis=0, keepdims=True), after, jnp.maximum(widest, after - window)

        zero = jnp.zeros((1, step), F32)
        total, seen, widest = lax.fori_loop(
            0, cells // step, body, (jnp.zeros((1, spots), F32), zero, zero)
        )
        compact_out[...] = mm(rbuf[...], hi_out[...]) + mm(rbuf[...], lo_out[...])
        extra_out[...] = jnp.zeros_like(extra_out)
        for h in range(spots // width):
            extra_out[h : h + 1, :] = total[:, h * width : (h + 1) * width]
        over = jnp.maximum((seen > cap).astype(F32), (widest > WINDOW).astype(F32))
        over = jnp.max(over, axis=1, keepdims=True)
        extra_out[EXTRA - 1 : EXTRA, :] = jnp.broadcast_to(over, (1, width))

    product(g, eth, etl, expr, extra_out, outs, obuf, sem)


def product(g, eth, etl, expr, extra, outs, obuf, sem):
    spots = eth.shape[0]
    count = len(outs)
    slot = lax.rem(g, 2)

    def put(n):
        return pltpu.make_async_copy(obuf.at[n % 2], outs[n], sem.at[n % 2])

    for n in range(2, count):

        @pl.when(g == n)
        def _():
            put(n - 2).wait()

    xh, xl = split(expr[...])
    obuf[slot, :spots, :] = mm3(eth[...], etl[...], xh, xl)
    obuf[slot, spots:, :] = extra[...]
    for n in range(count):

        @pl.when(g == n)
        def _():
            put(n).start()

    @pl.when(g == count - 1)
    def _():
        for n in range(count - 2, count):
            put(n).wait()


def more_kernel(sc, eth, etl, expr, extra, *refs):
    *outs, obuf, sem = refs
    views = [out.at[n] for out in outs for n in range(out.shape[0])]
    product(pl.program_id(0), eth, etl, expr, extra, views, obuf, sem)


def diagonal_kernel(sc, a, b, top, bottom):
    half = top.shape[0]
    top[...] = a[:half, :] + b[:half, :]
    bottom[...] = a[half:, :] + b[half:, :]


def merge_kernel(sc, a, b, low, high, one, two):
    half = high.shape[0]
    one[:half, :] = a[0, :half, :] + b[0, :half, :]
    one[half:, :] = (a[0, half:, :] + b[0, half:, :]) + low[...]
    two[:half, :] = (a[1, :half, :] + b[1, :half, :]) + high[...]
    two[half:, :] = a[1, half:, :] + b[1, half:, :]


def totals(extra_rows, spots):
    width = extra_rows.shape[1]
    cols = [
        jnp.broadcast_to(extra_rows[h : h + 1, :], (128, width)).T[:, :1] for h in range(spots // width)
    ]
    return jnp.concatenate(cols, axis=0)


def sums_kernel(sc, a, b, x, y, spatial, pred_out, sums_out, extra_out, over_out):
    spots = pred_out.shape[0]
    extra = (a[spots:, :] + b[spots:, :]) + (x[spots:, :] + y[spots:, :])
    extra_out[...] = extra
    over_out[0] = extra[EXTRA - 1, 0]
    z = totals(extra, spots)
    pred = ((a[:spots, :] + b[:spots, :]) + (x[:spots, :] + y[:spots, :])) / z
    pred_out[...] = pred
    spat = spatial[...]
    ids = lax.broadcasted_iota(I32, (spots, 1), 0) + sc[BASE]
    slide = slide_of(ids, sc)
    sums_out[...] = jnp.zeros_like(sums_out)
    for n, term in enumerate((pred * spat, pred * pred, spat * spat)):
        for k in range(4):
            sums_out[4 * n + k : 4 * n + k + 1, :] = jnp.sum(
                jnp.where(slide == k, term, 0.0), axis=0, keepdims=True
            )


def grad_kernel(sc, pred, spatial, extra, s0, s1, s2, s3, blk_out, cos_out):
    spots, width = pred.shape
    sums = (s0[...] + s1[...]) + (s2[...] + s3[...])
    a, b, c = sums[0:4, :], sums[4:8, :], sums[8:12, :]
    inv = lax.rsqrt(b) * lax.rsqrt(c)
    cos = a * inv
    ratio = cos / b
    cos_out[...] = cos
    ids = lax.broadcasted_iota(I32, (spots, 1), 0) + sc[BASE]
    slide = slide_of(ids, sc)
    spread_inv, spread_cos = inv[3:4, :], ratio[3:4, :]
    for k in range(3):
        spread_inv = jnp.where(slide == k, inv[k : k + 1, :], spread_inv)
        spread_cos = jnp.where(slide == k, ratio[k : k + 1, :], spread_cos)
    p = pred[...]
    grad = -(spatial[...] * spread_inv - p * spread_cos) / totals(extra[...], spots)
    blk_out[:spots, :] = grad
    dots = lax.dot_general(
        jnp.ones((8, width), F32), p * grad, (((1,), (1,)), ((), ())),
        precision=HIGH, preferred_element_type=F32,
    )
    blk_out[spots:, :] = jnp.zeros((EXTRA, width), F32)
    for h in range(spots // width):
        blk_out[spots + h : spots + h + 1, :] = dots[:1, h * width : (h + 1) * width]
    blk_out[spots + 4 : spots + 8, :] = cos


def fetch(g, steps, blocks, buf, sem):
    per = len(blocks) // steps

    def copies(s):
        return [pltpu.make_async_copy(blocks[s * per + n], buf.at[s, n], sem.at[s, n]) for n in range(per)]

    @pl.when(g == 0)
    def _():
        for s in range(steps):
            for c in copies(s):
                c.start()

    for s in range(steps):

        @pl.when(g == s)
        def _():
            for c in copies(s):
                c.wait()

    return buf.at[g]


def logit_kernel(steps, qs, sc, expr, *refs):
    blocks, refs = refs[: 2 * steps], refs[2 * steps :]
    final = qs[0] > 0
    if final:
        hi, lo, acc_in, dots_in, parts_in, out, loss_out, acc, dots, parts, buf, sem = refs
    else:
        acc, dots, parts, buf, sem = refs
    g = pl.program_id(0)
    cells, spots = acc.shape
    width = buf.shape[3]
    got = fetch(g, steps, blocks, buf, sem)

    @pl.when(g == 0)
    def _():
        dots[...] = dots_in[...] if final else jnp.zeros_like(dots)
        if final:
            parts[...] = parts_in[...]
        else:
            parts[...] = jnp.zeros_like(parts)

    parity = lax.rem(sc[CELL], 2)

    def add(first):
        halves = []
        for side in range(2):
            start = pl.multiple_of(jnp.where(parity == side, 0, width), width)
            gh, gl = split(got[side, :spots, :])
            dots[...] += got[side, spots:, :]
            sums = jnp.sum(got[side, spots:, :], axis=1, keepdims=True)
            parts[sc[CELL] ^ (2 * (g + qs[0]) + side)] = jnp.broadcast_to(sums, parts.shape[1:])
            halves.append((start, gh, gl))

        def body(t, _):
            rows = block_rows(t, 256)
            value = None
            for start, gh, gl in halves:
                xh, xl = split(expr[rows, pl.ds(start, width)])
                term = mm3(xh, xl, gh, gl, ((1,), (1,)))
                value = term if value is None else value + term
            if not first:
                acc[rows, :] += value
            elif final:
                acc[rows, :] = acc_in[rows, :] + value
            else:
                acc[rows, :] = value
            return 0

        lax.fori_loop(0, cells // 256, body, 0, unroll=True)

    @pl.when(g == 0)
    def _():
        add(True)

    @pl.when(g > 0)
    def _():
        add(False)

    if final:

        @pl.when(g == steps - 1)
        def _():
            row = jnp.concatenate([dots[h : h + 1, :] for h in range(spots // width)], axis=1)
            e = hi[...].astype(F32) + lo[...].astype(F32)
            out[...] = e * (acc[...] - row)
            total = parts[0]
            for n in range(1, parts.shape[0]):
                total = total + parts[n]
            for k in range(4):
                loss_out[k] = -total[4 + k, 0]


def halves_kernel(sc, compact, far1, far_n, far_e, far_m, far_f, hi_out, lo_out):
    spots = compact.shape[1]
    middle = (sc[BASE] == spots) | (sc[BASE] == 2 * spots)
    two = jnp.where(middle, far_n[...], far_e[...])
    three = jnp.where(middle, far_m[...], far_f[...])
    for n, value in enumerate((compact[...], far1[...], two, three)):
        hi_out[n], lo_out[n] = split(value)


def rows_kernel(steps, alias, sc, table, *refs):
    blocks, refs = refs[: 8 * steps], refs[8 * steps :]
    (maps_hi, maps_lo, place), refs = refs[:3], refs[3 + alias :]
    out, buf, sem, mh, ml, msem, gh, gl, res, sh, sl = refs
    g = pl.program_id(0)
    cells = out.shape[0]
    cap, spots = mh.shape[1:]
    width = buf.shape[3]
    half = spots // 2

    def bring(s, n):
        return pltpu.make_async_copy(blocks[8 * s + n], buf.at[s, n], sem.at[s, n])

    def bring_maps(n):
        return [
            pltpu.make_async_copy(maps_hi.at[n], mh.at[n], msem.at[n, 0]),
            pltpu.make_async_copy(maps_lo.at[n], ml.at[n], msem.at[n, 1]),
        ]

    own = sc[BASE] // spots

    @pl.when(g == 0)
    def _():
        for s in range(steps):
            for n in range(4):
                if s == 0:
                    for c in bring_maps(n):
                        c.start()
                for side in range(2):
                    bring(s, 2 * n + side).start()

    parity = lax.rem(sc[CELL], 2)

    def layer_body(layer, _):
        partner = layer ^ own
        for side in range(2):
            n = 2 * partner + side
            pltpu.make_async_copy(blocks[0], buf.at[g, n], sem.at[g, n]).wait()

        @pl.when(g == 0)
        def _():
            for c in bring_maps(partner):
                c.wait()

        for side in range(2):
            start = pl.multiple_of(jnp.where(parity == side, 0, width), width)
            hi, lo = split(buf[g, 2 * partner + side, :spots, :])
            gh[:, pl.ds(start, width)] = hi
            gl[:, pl.ds(start, width)] = lo
        base = layer * spots
        low, low_end = slide_of(base, sc), slide_of(base + half - 1, sc)
        high, high_end = slide_of(base + half, sc), slide_of(base + spots - 1, sc)
        before = jnp.where(layer == 0, -1, slide_of(base - 1, sc))

        def put(k, value):
            res[k] = jnp.where(k > before, 0.0, res[k]) + value

        @pl.when(low == high_end)
        def _():
            put(low, mm3(mh[partner], ml[partner], gh[...], gl[...]))

        def slide_body(k, _):
            in_low, in_high = k <= low_end, k >= high

            def part(first, count):
                cols = pl.ds(first, count)
                ids = lax.broadcasted_iota(I32, (1, count), 1) + (base + first)
                keep = (slide_of(ids, sc) == k).astype(F32).astype(BF16)
                put(k, mm3(mh[partner, :, cols] * keep, ml[partner, :, cols] * keep, gh[cols, :], gl[cols, :]))

            @pl.when(in_low & in_high)
            def _():
                part(0, spots)

            @pl.when(jnp.logical_not(in_low & in_high))
            def _():
                part(pl.multiple_of(jnp.where(in_low, 0, half), half), half)

            return 0

        lax.fori_loop(low, jnp.where(low == high_end, low, high_end + 1), slide_body, 0)
        return 0

    lax.fori_loop(0, 4, layer_body, 0)
    slots = lax.broadcasted_iota(I32, (1, 4 * WINDOW), 1)

    def place_body(t, _):
        rows = block_rows(t, 128)
        for k in range(4):
            window = pl.ds(pl.multiple_of(table[t, k], 8), WINDOW)
            hi, lo = split(res[k, window, :])
            sh[k * WINDOW : (k + 1) * WINDOW, :] = hi
            sl[k * WINDOW : (k + 1) * WINDOW, :] = lo
        pick = (place[rows, :] == slots).astype(F32).astype(BF16)
        out[rows, :] = mm(pick, sh[...]) + mm(pick, sl[...])
        return 0

    lax.fori_loop(0, cells // 128, place_body, 0)


def expr_kernel(steps, layers, near, alias, sc, *refs):
    refs = list(refs)
    blocks = [refs.pop(0) for _ in range(2 * layers * steps)]
    maps = [(refs.pop(0), refs.pop(0)) for _ in range(layers)]
    acc = refs.pop(0) if near else None
    if alias:
        refs.pop(0)
    out, buf, sem = refs
    g = pl.program_id(0)
    cells, spots = maps[0][0].shape
    width = buf.shape[3]
    got = fetch(g, steps, blocks, buf, sem)
    parity = lax.rem(sc[CELL], 2)
    for side in range(2):
        start = pl.multiple_of(jnp.where(parity == side, 0, width), width)
        grads = [split(got[2 * n + side, :spots, :]) for n in range(layers)]

        def body(t, _):
            rows = block_rows(t, 256)
            value = None
            for (mh, ml), (gh, gl) in zip(maps, grads):
                term = mm3(mh[rows, :], ml[rows, :], gh, gl)
                value = term if value is None else value + term
            if acc is not None:
                value = acc[rows, pl.ds(start, width)] + value
            out[rows, pl.ds(start, width)] = value
            return 0

        lax.fori_loop(0, cells // 256, body, 0, unroll=True)


def tie(x, *others):
    return lax.optimization_barrier((x, *others))[0]


def whole(shape):
    return pl.BlockSpec(shape, lambda *_: (0,) * len(shape))


ANY = pl.BlockSpec(memory_space=pl.ANY)
HBM = pl.BlockSpec(memory_space=pltpu.HBM)
SMEM = pl.BlockSpec(memory_space=pltpu.SMEM)


def call(kernel, sc, args, in_specs, outs, out_specs, grid=(1,), scratch=(), flops=0, name=None, alias=None, size=None):
    if size is None:
        size = sum(x.size * x.dtype.itemsize for x in (*args, *jax.tree.leaves(outs)))
    return pl.pallas_call(
        kernel,
        out_shape=outs,
        grid_spec=pltpu.PrefetchScalarGridSpec(
            num_scalar_prefetch=len(sc), grid=grid, in_specs=in_specs, out_specs=out_specs, scratch_shapes=scratch
        ),
        cost_estimate=pl.CostEstimate(flops=flops, bytes_accessed=size, transcendentals=0),
        input_output_aliases=alias or {},
        name=name,
    )(*sc, *args)


def fast(logits, expression, spatial, spot_counts, cell_mask, cell_slide):
    cells, spots = logits.shape
    genes = expression.shape[1]
    n_cell, n_spot = lax.axis_size("cell"), lax.axis_size("spot")
    width = genes // n_cell
    half, rows = spots // 2, spots + EXTRA
    ci, zi = lax.axis_index("cell"), lax.axis_index("spot")
    places = [ci, *((zi ^ k) * spots for k in range(n_spot))]
    sc = (jnp.concatenate([spot_counts, jnp.stack(places), jnp.array(BLOCKS, I32)]).astype(I32),)
    sds = jax.ShapeDtypeStruct
    block_sds, block_spec = sds((rows, width), F32), whole((rows, width))

    put_scratch = [pltpu.VMEM((2, rows, width), F32), pltpu.SemaphoreType.DMA((2,))]

    def cell_swap(x, bit):
        return lax.ppermute(x, "cell", [(i, i ^ bit) for i in range(n_cell)])

    def spot_swap(x, k):
        return lax.ppermute(x, "spot", [(i, i ^ k) for i in range(n_spot)])

    def spot_move(x, moves):
        return lax.ppermute(x, "spot", moves)

    def genes_spec(first):
        return pl.BlockSpec((cells, width), lambda g, sc, *_: (0, sc[CELL] ^ sc[ORDER + first + g]))

    hi, lo, eth, etl, compact, extra, place, table, b7, b6 = call(
        first_kernel, sc, (logits, cell_mask.reshape(-1, 128), cell_slide.reshape(-1, 128), expression),
        [whole((cells, spots)), whole((cells // 128, 128)), whole((cells // 128, 128)), genes_spec(0)],
        (
            sds((cells, spots), BF16), sds((cells, spots), BF16), sds((spots, cells), BF16), sds((spots, cells), BF16),
            sds((CAPACITY, spots), F32), sds((EXTRA, width), F32), sds((cells, 1), I32), sds((cells // 128, 128), I32),
            block_sds, block_sds,
        ),
        (
            whole((cells, spots)), whole((cells, spots)), whole((spots, cells)), whole((spots, cells)),
            whole((CAPACITY, spots)), whole((EXTRA, width)), whole((cells, 1)), whole((cells // 128, 128)), ANY, ANY,
        ),
        grid=(2,), scratch=[pltpu.VMEM((CAPACITY, cells), BF16), *put_scratch],
        flops=4 * cells * spots * CAPACITY + 12 * cells * spots * width, name="first",
    )

    def products(first, parts, extra, size=None):
        count = sum(parts)
        return call(
            more_kernel, sc, (eth, etl, expression, extra),
            [whole((spots, cells)), whole((spots, cells)), genes_spec(first), whole((EXTRA, width))],
            tuple(sds((n, rows, width), F32) for n in parts), (ANY,) * len(parts), scratch=put_scratch,
            grid=(count,), flops=0 if size == 0 else 6 * cells * spots * width * count, name="more", size=size,
        )

    far_m, far1 = spot_move(compact, MIDDLE), spot_swap(compact, 1)
    top3, low3 = call(
        diagonal_kernel, sc, (b6, cell_swap(b7, 1)), [block_spec] * 2,
        (sds((half, width), F32), sds((rows - half, width), F32)),
        (whole((half, width)), whole((rows - half, width))), name="diagonal", size=0,
    )
    in_top, in_low = cell_swap(top3, 2), cell_swap(low3, 4)
    (odd,) = products(2, (3,), tie(extra, top3), 0)
    far_n, far_e = spot_move(tie(far1, far_m, odd), MIDDLE), spot_move(tie(far_m, far1, odd), OUTWARD)
    in_odd = cell_swap(tie(odd, far1, far_m, in_top, in_low), 1)
    (even,) = products(5, (3,), tie(extra, odd, far1, far_m))
    three_blocks = whole((3, rows, width))
    one, two = call(
        merge_kernel, sc, (even, in_odd, in_low, in_top),
        [three_blocks, three_blocks, whole((rows - half, width)), whole((half, width))],
        (block_sds, block_sds), (block_spec, block_spec), name="merge",
    )
    in_x, in_y = cell_swap(one, 2), cell_swap(two, 4)
    far_f = spot_move(tie(far_n, far_e, one), OUTWARD)
    own_spatial = pl.BlockSpec((spots, width), lambda g, sc, *_: (0, sc[CELL]))
    small = whole((16, width))
    one_block = pl.BlockSpec((None, rows, width), lambda *_: (2, 0, 0))
    predicted, sums, extra_all, over = call(
        sums_kernel, sc, (even, in_odd, in_x, in_y, spatial),
        [one_block, one_block, block_spec, block_spec, own_spatial],
        (sds((spots, width), F32), sds((16, width), F32), sds((EXTRA, width), F32), sds((1,), F32)),
        (whole((spots, width)), small, whole((EXTRA, width)), SMEM), flops=5 * 10**9, name="sums",
    )
    all_sums = [sums, *(spot_swap(tie(sums, far_f), k) for k in range(1, n_spot))]
    maps_shape = (n_spot, CAPACITY, spots)
    comps = call(
        halves_kernel, sc, (tie(compact, sums), far1, far_n, far_e, far_m, far_f), [whole((CAPACITY, spots))] * 6,
        (sds(maps_shape, BF16),) * 2, (whole(maps_shape),) * 2, name="halves",
    )
    block, cosines = call(
        grad_kernel, sc, (tie(predicted, comps[0]), spatial, extra_all, *all_sums),
        [whole((spots, width)), own_spatial, whole((EXTRA, width))] + [small] * n_spot,
        (block_sds, sds((4, width), F32)), (block_spec, whole((4, width))), name="grad",
    )

    def pair(g, sc, qs):
        q = qs[0]
        for n, value in enumerate(qs):
            q = jnp.where(g == n, value, q) if n else q
        return (sc[CELL] // 2) ^ q

    def logit_part(got, qs, sums=None):
        blocks = [x for q in qs for x in got[q]]
        sizes = ((cells, spots), (EXTRA, width), (n_cell, EXTRA, 128))
        args = [expression, *blocks]
        specs = [
            pl.BlockSpec((cells, 2 * width), lambda g, sc, *_: (0, pair(g, sc, qs))), *[ANY] * len(blocks),
        ]
        outs, scratch = sizes, []
        if sums is not None:
            args += [hi, lo, *sums]
            specs += [whole((cells, spots)), whole((cells, spots)), *map(whole, sizes)]
            outs, scratch = ((cells, spots), (4,)), [pltpu.VMEM(size, F32) for size in sizes]
        steps = len(qs)
        return call(
            functools.partial(logit_kernel, steps, qs), sc, args, specs,
            tuple(sds(size, F32) for size in outs), tuple(whole(o) if len(o) > 1 else SMEM for o in outs), grid=(steps,),
            scratch=[*scratch, pltpu.VMEM((steps, 2, rows, width), F32), pltpu.SemaphoreType.DMA((steps, 2))],
            flops=12 * cells * spots * width * steps, name="logit",
        )

    def rows_part(gots, comps, qs, onto=None, space=ANY):
        blocks = [x for q in qs for got in gots for x in got[q]]
        args = [*blocks, *comps, place]
        specs = [space] * (len(blocks) + 2) + [whole((cells, 1))]
        alias = None
        if onto is not None:
            alias = {len(args) + 2: 0}
            args.append(onto)
            specs.append(ANY)
        steps = len(qs)
        return call(
            functools.partial(rows_kernel, steps, int(onto is not None)), (*sc, table), args, specs,
            sds((cells, genes), F32), pl.BlockSpec((cells, 2 * width), lambda g, sc, *_: (0, pair(g, sc, qs))),
            grid=(steps,), alias=alias,
            scratch=[
                pltpu.VMEM((steps, 8, rows, width), F32), pltpu.SemaphoreType.DMA((steps, 8)),
                pltpu.VMEM((4, CAPACITY, spots), BF16), pltpu.VMEM((4, CAPACITY, spots), BF16),
                pltpu.SemaphoreType.DMA((4, 2)),
                pltpu.VMEM((spots, 2 * width), BF16), pltpu.VMEM((spots, 2 * width), BF16),
                pltpu.VMEM((4, CAPACITY, 2 * width), F32),
                pltpu.VMEM((4 * WINDOW, 2 * width), BF16), pltpu.VMEM((4 * WINDOW, 2 * width), BF16),
            ],
            name="rows",
        )

    def expr_part(gots, maps, qs, near=None, final=False, onto=None):
        blocks = [x for q in qs for got in gots for x in got[q]]
        args = [*blocks, *(m for pairs in maps for m in pairs)]
        specs = [ANY] * len(blocks) + [whole((cells, spots))] * (2 * len(maps))
        columns = pl.BlockSpec((cells, 2 * width), lambda g, sc, *_: (0, pair(g, sc, qs)))
        steps_spec = pl.BlockSpec((None, cells, 2 * width), lambda g, sc, *_: (g, 0, 0))
        alias = None
        if near is not None:
            args.append(near)
            specs.append(steps_spec)
        if onto is not None:
            alias = {len(args) + 1: 0}
            args.append(onto)
            specs.append(ANY)
        out = sds((cells, genes) if final else (len(qs), cells, 2 * width), F32)
        scratch = [
            pltpu.VMEM((len(qs), 2 * len(maps), rows, width), F32),
            pltpu.SemaphoreType.DMA((len(qs), 2 * len(maps))),
        ]
        return call(
            functools.partial(expr_kernel, len(qs), len(maps), near is not None, onto is not None), sc, args, specs,
            out, columns if final else steps_spec, grid=(len(qs),), scratch=scratch, alias=alias,
            flops=6 * cells * spots * 2 * width * len(qs) * len(maps), name="expr",
        )

    def cores(x, *others):
        return (x, cell_swap(tie(x, *others) if others else x, 1))

    o_x, o_y = cell_swap(block, 2), cell_swap(block, 4)
    z1, mid = spot_swap(block, 1), spot_move(block, MIDDLE)
    got_o = {0: cores(block), 1: cores(o_x)}
    a_x, o_d = cell_swap(tie(z1, o_x), 2), cell_swap(tie(o_x, o_y, z1), 4)
    mid2, end2 = spot_move(tie(z1, mid), MIDDLE), spot_move(tie(mid, z1), OUTWARD)
    part = logit_part(got_o, (0, 1))
    z2 = tie(mid2, part[0]) + end2
    a_y = cell_swap(tie(z1, o_d, part[0]), 4)
    c_x = cell_swap(tie(z2, a_x, part[0]), 2)
    end3 = spot_move(tie(mid2, end2, part[0]), OUTWARD)
    got_o[2], got_o[3] = cores(o_y, part[0], a_x, z2), cores(o_d, part[0], a_x, z2)
    logit_grad, losses = logit_part(got_o, (2, 3), part)
    z3 = tie(mid, logit_grad) + end3
    c_y = cell_swap(tie(z2, a_y, logit_grad), 4)
    d_x = cell_swap(tie(z3, c_x, logit_grad), 2)
    early = (got_o[2][1], got_o[3][1])
    got_a, got_c = {0: cores(z1, *early)}, {0: cores(z2, *early)}
    got_d = {0: cores(z3, got_a[0][1], got_c[0][1], a_y, c_x)}
    gots = (got_o, got_a, got_c, got_d)
    body = rows_part(gots, comps, (0,))
    a_d, d_y = cell_swap(tie(a_y, d_x, body), 2), cell_swap(tie(z3, c_y, body), 4)
    early = (logit_grad, got_d[0][1])
    got_a[1], got_c[1] = cores(a_x, *early), cores(c_x, *early)
    got_d[1] = cores(d_x, got_a[1][1], got_c[1][1], body, c_y)
    body = rows_part(gots, comps, (1,), body)
    d_d, c_d = cell_swap(tie(d_y, a_d, body), 2), cell_swap(tie(c_x, d_y, body), 4)
    got_a[2], got_c[2] = cores(a_y, got_d[1][1]), cores(c_y, got_d[1][1])
    got_d[2] = cores(d_y, got_a[2][1], got_c[2][1], a_d, body)
    got_a[3] = cores(a_d, body, got_d[2][1])
    body = rows_part(gots, comps, (2,), body)
    got_c[3], got_d[3] = cores(c_d, body, got_a[3][1]), cores(d_d, body, got_a[3][1])

    def direct(operands):
        body, last = operands[:2]
        return rows_part(last, comps, (3,), body, HBM)

    def exchange(operands):
        term = expr_part((operands[2],), ((hi, lo),), (0, 1, 2, 3), final=True)
        one, two, three = (spot_swap(term, k) for k in (1, 2, 3))
        return (term + one) + (two + three)

    expression_grad = lax.cond(
        over[0] > 0, exchange, direct, (body, [{3: got[3]} for got in gots], got_o)
    )

    return losses, predicted, cosines, logit_grad, expression_grad


def plain(logits, expression, spatial, spot_counts, cell_mask, cell_slide):
    spot_cols = logits.shape[1]
    gene_total = expression.shape[1]
    slide_total = spot_counts.shape[0]
    gene_rows = gene_total // lax.axis_size("cell")
    gene_start = lax.axis_index("cell") * gene_rows
    slide_ends = jnp.cumsum(spot_counts)
    spot_ids = lax.axis_index("spot") * spot_cols + jnp.arange(spot_cols, dtype=I32)
    spot_slide = jnp.sum((spot_ids[:, None] >= slide_ends[None, : slide_total - 1]).astype(I32), axis=1)
    member = (cell_mask[:, None] == 1) & (cell_slide[:, None] == spot_slide[None, :])
    onehot = (spot_slide[:, None] == jnp.arange(slide_total, dtype=I32)[None, :]).astype(F32)
    exponent = jnp.where(member, jnp.exp(logits), 0.0)
    column_total = lax.psum(jnp.sum(exponent, axis=0), "cell")
    mapping = exponent / column_total[None, :]
    predicted = lax.psum_scatter(
        lax.dot_general(expression, mapping, (((0,), (0,)), ((), ())), precision=HIGH),
        "cell", scatter_dimension=0, tiled=True,
    ).T
    spatial_own = lax.dynamic_slice_in_dim(spatial, gene_start, gene_rows, 1)
    sum_a, sum_b, sum_c = lax.psum(
        tuple(
            jnp.dot(onehot.T, t, precision=HIGH)
            for t in (predicted * spatial_own, predicted * predicted, spatial_own * spatial_own)
        ),
        "spot",
    )
    inverse_norms = lax.rsqrt(sum_b) * lax.rsqrt(sum_c)
    cosines = sum_a * inverse_norms
    spread_inv = jnp.dot(onehot, inverse_norms, precision=HIGH)
    spread_cos = jnp.dot(onehot, cosines / sum_b, precision=HIGH)
    pred_grad = -(spatial_own * spread_inv - predicted * spread_cos)
    losses, column_dot = lax.psum((-jnp.sum(cosines, axis=1), jnp.sum(predicted * pred_grad, axis=1)), "cell")
    grad_full = lax.all_gather(pred_grad, "cell", axis=1, tiled=True)
    map_grad = lax.dot_general(expression, grad_full, (((1,), (1,)), ((), ())), precision=HIGH)
    logit_grad = mapping * (map_grad - column_dot[None, :])
    expression_grad = lax.psum(jnp.dot(mapping, grad_full, precision=HIGH), "spot")
    return losses, predicted, cosines, logit_grad, expression_grad


def solution(mesh):
    small = mesh.shape["cell"] == 8 and mesh.shape["spot"] == 4
    return jax.shard_map(
        fast if small else plain,
        mesh=mesh,
        in_specs=(P("cell", "spot"), P("cell", None), P("spot", None), P(), P("cell"), P("cell")),
        out_specs=(P(), P("spot", "cell"), P(None, "cell"), P("cell", "spot"), P("cell", None)),
        check_vma=False,
    )
```

```python
import functools

import jax
import jax.numpy as jnp
from jax import lax
from jax.experimental import pallas as pl
from jax.experimental.pallas import tpu as pltpu
from jax.sharding import PartitionSpec as P

HIGH = lax.Precision.HIGHEST
F32, BF16, I32 = jnp.float32, jnp.bfloat16, jnp.int32
CAPACITY = 304
EXTRA = 8
WINDOW = 64
MIDDLE = ((1, 2), (2, 1))
OUTWARD = ((1, 0), (2, 3))
COUNTS, CELL, BASE, ORDER = 0, 4, 5, 9
BLOCKS = (7, 6, 3, 5, 1, 2, 4, 0)


def split(x):
    hi = x.astype(BF16)
    return hi, (x - hi.astype(F32)).astype(BF16)


def mm(a, b, dims=((1,), (0,))):
    return lax.dot_general(a, b, (dims, ((), ())), preferred_element_type=F32)


def mm3(ah, al, bh, bl, dims=((1,), (0,))):
    return mm(ah, bh, dims) + (mm(ah, bl, dims) + mm(al, bh, dims))


def slide_of(ids, sc):
    end, slide = 0, 0
    for k in range(3):
        end = end + sc[COUNTS + k]
        slide = slide + (ids >= end).astype(I32)
    return slide


def block_rows(t, step):
    return pl.ds(pl.multiple_of(t * step, step), step)


def first_kernel(sc, logits, mask, slide, expr, *refs):
    *kept, compact_out, extra_out, place_out, table_out = refs[:8]
    *outs, rbuf, obuf, sem, hi_out, lo_out, eth, etl, ksem = refs[8:]
    cells, spots = logits.shape
    cap, width = compact_out.shape[0], extra_out.shape[1]
    step = 128
    g = pl.program_id(0)

    @pl.when(g == 0)
    def _():
        lane = lax.broadcasted_iota(I32, (1, spots), 1) + sc[BASE]
        spot_slide = slide_of(lane, sc)
        lanes = lax.broadcasted_iota(I32, (1, step), 1).astype(F32)
        lower = (
            lax.broadcasted_iota(I32, (step, step), 0) > lax.broadcasted_iota(I32, (step, step), 1)
        ).astype(BF16)

        def body(t, carry):
            total, seen, widest = carry
            rows = block_rows(t, step)
            one = pl.ds(t, 1)
            own_row = jnp.where(mask[one, :] == 1, slide[one, :], -1).astype(F32)
            own = jnp.broadcast_to(own_row, (step, step)).T[:, :1]
            e = jnp.where(own.astype(I32) == spot_slide, jnp.exp(logits[rows, :]), 0.0)
            hi, lo = split(e)
            e = hi.astype(F32) + lo.astype(F32)
            hi, lo = split(e)
            hi_out[rows, :] = hi
            lo_out[rows, :] = lo
            hit, lit = split(e.T)
            eth[:, rows] = hit
            etl[:, rows] = lit
            onehot = (own == lanes).astype(F32)
            before = mm(lower, onehot.astype(BF16)) + seen
            rank = jnp.sum(onehot * before, axis=1, keepdims=True)
            rank = jnp.where(own >= 0, rank, -1.0)
            window = jnp.minimum((seen.astype(I32) // 8) * 8, cap - WINDOW)
            table_out[one, :] = window
            window = window.astype(F32)
            local = jnp.sum(onehot * (before - window), axis=1, keepdims=True) + WINDOW * own
            place_out[rows, :] = jnp.where(own >= 0, local, -1.0).astype(I32)
            row = jnp.broadcast_to(rank, (step, step)).T[:1, :].astype(I32)
            rbuf[:, rows] = (lax.broadcasted_iota(I32, (cap, step), 0) == row).astype(F32).astype(BF16)
            after = seen + jnp.sum(onehot, axis=0, keepdims=True)
            return total + jnp.sum(e, axis=0, keepdims=True), after, jnp.maximum(widest, after - window)

        zero = jnp.zeros((1, step), F32)
        total, seen, widest = lax.fori_loop(
            0, cells // step, body, (jnp.zeros((1, spots), F32), zero, zero)
        )
        compact_out[...] = mm(rbuf[...], hi_out[...]) + mm(rbuf[...], lo_out[...])
        extra_out[...] = jnp.zeros_like(extra_out)
        for h in range(spots // width):
            extra_out[h : h + 1, :] = total[:, h * width : (h + 1) * width]
        over = jnp.maximum((seen > cap).astype(F32), (widest > WINDOW).astype(F32))
        over = jnp.max(over, axis=1, keepdims=True)
        extra_out[EXTRA - 1 : EXTRA, :] = jnp.broadcast_to(over, (1, width))
        load(list(zip((hi_out, lo_out, eth, etl), kept)), ksem)

    product(g, eth, etl, expr, extra_out, outs, obuf, sem)

    @pl.when(g == 1)
    def _():
        for n, (source, place) in enumerate(zip((hi_out, lo_out, eth, etl), kept)):
            pltpu.make_async_copy(source, place, ksem.at[n]).wait()


def product(g, eth, etl, expr, extra, outs, obuf, sem):
    spots = eth.shape[0]
    count = len(outs)
    slot = lax.rem(g, 2)

    def put(n):
        return pltpu.make_async_copy(obuf.at[n % 2], outs[n], sem.at[n % 2])

    for n in range(2, count):

        @pl.when(g == n)
        def _():
            put(n - 2).wait()

    xh, xl = split(expr[...])
    obuf[slot, :spots, :] = mm3(eth[...], etl[...], xh, xl)
    obuf[slot, spots:, :] = extra[...]
    for n in range(count):

        @pl.when(g == n)
        def _():
            put(n).start()

    @pl.when(g == count - 1)
    def _():
        for n in range(count - 2, count):
            put(n).wait()


def more_kernel(sc, eth, etl, expr, extra, *refs):
    *outs, obuf, sem = refs
    views = [out.at[n] for out in outs for n in range(out.shape[0])]
    product(pl.program_id(0), eth, etl, expr, extra, views, obuf, sem)


def load(pairs, sem):
    copies = [pltpu.make_async_copy(source, place, sem.at[n]) for n, (source, place) in enumerate(pairs)]
    for c in copies:
        c.start()
    return copies


def diagonal_kernel(sc, a, b, top, bottom, abuf, bbuf, sem):
    half = top.shape[0]
    upper, lower = pl.ds(0, half), pl.ds(half, bottom.shape[0])
    parts = [(x.at[r], y.at[r]) for r in (upper, lower) for x, y in ((a, abuf), (b, bbuf))]
    copies = load(parts, sem)
    for c in copies[:2]:
        c.wait()
    top[...] = abuf[upper, :] + bbuf[upper, :]
    for c in copies[2:]:
        c.wait()
    bottom[...] = abuf[lower, :] + bbuf[lower, :]


def merge_kernel(sc, a, b, low, high, one, two, abuf, bbuf, lbuf, hbuf, sem):
    half = high.shape[0]
    copies = load(
        [(a.at[0], abuf.at[0]), (b.at[0], bbuf.at[0]), (low, lbuf), (a.at[1], abuf.at[1]), (b.at[1], bbuf.at[1]), (high, hbuf)],
        sem,
    )
    for c in copies[:3]:
        c.wait()
    one[:half, :] = abuf[0, :half, :] + bbuf[0, :half, :]
    one[half:, :] = (abuf[0, half:, :] + bbuf[0, half:, :]) + lbuf[...]
    for c in copies[3:]:
        c.wait()
    two[:half, :] = (abuf[1, :half, :] + bbuf[1, :half, :]) + hbuf[...]
    two[half:, :] = abuf[1, half:, :] + bbuf[1, half:, :]


def totals(extra_rows, spots):
    width = extra_rows.shape[1]
    cols = [
        jnp.broadcast_to(extra_rows[h : h + 1, :], (128, width)).T[:, :1] for h in range(spots // width)
    ]
    return jnp.concatenate(cols, axis=0)


def sums_kernel(sc, a, b, x, y, spatial, pred_out, sums_out, extra_out, over_out):
    spots = pred_out.shape[0]
    extra = (a[spots:, :] + b[spots:, :]) + (x[spots:, :] + y[spots:, :])
    extra_out[...] = extra
    over_out[0] = extra[EXTRA - 1, 0]
    z = totals(extra, spots)
    pred = ((a[:spots, :] + b[:spots, :]) + (x[:spots, :] + y[:spots, :])) / z
    pred_out[...] = pred
    spat = spatial[...]
    ids = lax.broadcasted_iota(I32, (spots, 1), 0) + sc[BASE]
    slide = slide_of(ids, sc)
    sums_out[...] = jnp.zeros_like(sums_out)
    for n, term in enumerate((pred * spat, pred * pred, spat * spat)):
        for k in range(4):
            sums_out[4 * n + k : 4 * n + k + 1, :] = jnp.sum(
                jnp.where(slide == k, term, 0.0), axis=0, keepdims=True
            )


def grad_kernel(sc, pred, spatial, extra, s0, s1, s2, s3, blk_out, cos_out):
    spots, width = pred.shape
    sums = (s0[...] + s1[...]) + (s2[...] + s3[...])
    a, b, c = sums[0:4, :], sums[4:8, :], sums[8:12, :]
    inv = lax.rsqrt(b) * lax.rsqrt(c)
    cos = a * inv
    ratio = cos / b
    cos_out[...] = cos
    ids = lax.broadcasted_iota(I32, (spots, 1), 0) + sc[BASE]
    slide = slide_of(ids, sc)
    spread_inv, spread_cos = inv[3:4, :], ratio[3:4, :]
    for k in range(3):
        spread_inv = jnp.where(slide == k, inv[k : k + 1, :], spread_inv)
        spread_cos = jnp.where(slide == k, ratio[k : k + 1, :], spread_cos)
    p = pred[...]
    grad = -(spatial[...] * spread_inv - p * spread_cos) / totals(extra[...], spots)
    blk_out[:spots, :] = grad
    dots = lax.dot_general(
        jnp.ones((8, width), F32), p * grad, (((1,), (1,)), ((), ())),
        precision=HIGH, preferred_element_type=F32,
    )
    blk_out[spots:, :] = jnp.zeros((EXTRA, width), F32)
    for h in range(spots // width):
        blk_out[spots + h : spots + h + 1, :] = dots[:1, h * width : (h + 1) * width]
    blk_out[spots + 4 : spots + 8, :] = cos


def fetch(g, steps, blocks, buf, sem):
    per = len(blocks) // steps

    def copies(s):
        return [pltpu.make_async_copy(blocks[s * per + n], buf.at[s, n], sem.at[s, n]) for n in range(per)]

    @pl.when(g == 0)
    def _():
        for s in range(steps):
            for c in copies(s):
                c.start()

    for s in range(steps):

        @pl.when(g == s)
        def _():
            for c in copies(s):
                c.wait()

    return buf.at[g]


def logit_kernel(steps, qs, sc, expr, *refs):
    blocks, refs = refs[: 2 * steps], refs[2 * steps :]
    final = qs[0] > 0
    if final:
        hi, lo, acc_in, dots_in, parts_in, out, loss_out, acc, dots, parts, buf, sem = refs
    else:
        acc, dots, parts, buf, sem = refs
    g = pl.program_id(0)
    cells, spots = acc.shape
    width = buf.shape[3]
    got = fetch(g, steps, blocks, buf, sem)

    @pl.when(g == 0)
    def _():
        dots[...] = dots_in[...] if final else jnp.zeros_like(dots)
        if final:
            parts[...] = parts_in[...]
        else:
            parts[...] = jnp.zeros_like(parts)

    parity = lax.rem(sc[CELL], 2)

    def add(first):
        halves = []
        for side in range(2):
            start = pl.multiple_of(jnp.where(parity == side, 0, width), width)
            gh, gl = split(got[side, :spots, :])
            dots[...] += got[side, spots:, :]
            sums = jnp.sum(got[side, spots:, :], axis=1, keepdims=True)
            parts[sc[CELL] ^ (2 * (g + qs[0]) + side)] = jnp.broadcast_to(sums, parts.shape[1:])
            halves.append((start, gh, gl))

        def body(t, _):
            rows = block_rows(t, 256)
            value = None
            for start, gh, gl in halves:
                xh, xl = split(expr[rows, pl.ds(start, width)])
                term = mm3(xh, xl, gh, gl, ((1,), (1,)))
                value = term if value is None else value + term
            if not first:
                acc[rows, :] += value
            elif final:
                acc[rows, :] = acc_in[rows, :] + value
            else:
                acc[rows, :] = value
            return 0

        lax.fori_loop(0, cells // 256, body, 0, unroll=True)

    @pl.when(g == 0)
    def _():
        add(True)

    @pl.when(g > 0)
    def _():
        add(False)

    if final:

        @pl.when(g == steps - 1)
        def _():
            row = jnp.concatenate([dots[h : h + 1, :] for h in range(spots // width)], axis=1)
            e = hi[...].astype(F32) + lo[...].astype(F32)
            out[...] = e * (acc[...] - row)
            total = parts[0]
            for n in range(1, parts.shape[0]):
                total = total + parts[n]
            for k in range(4):
                loss_out[k] = -total[4 + k, 0]


def halves_kernel(sc, compact, far1, far_n, far_e, far_m, far_f, hi_out, lo_out):
    spots = compact.shape[1]
    middle = (sc[BASE] == spots) | (sc[BASE] == 2 * spots)
    two = jnp.where(middle, far_n[...], far_e[...])
    three = jnp.where(middle, far_m[...], far_f[...])
    for n, value in enumerate((compact[...], far1[...], two, three)):
        hi_out[n], lo_out[n] = split(value)


def rows_kernel(steps, alias, sc, table, *refs):
    blocks, refs = refs[: 8 * steps], refs[8 * steps :]
    (maps_hi, maps_lo, place), refs = refs[:3], refs[3 + alias :]
    out, buf, sem, mh, ml, msem, gh, gl, res, sh, sl = refs
    g = pl.program_id(0)
    cells = out.shape[0]
    cap, spots = mh.shape[1:]
    width = buf.shape[3]
    half = spots // 2

    def bring(s, n):
        return pltpu.make_async_copy(blocks[8 * s + n], buf.at[s, n], sem.at[s, n])

    def bring_maps(n):
        return [
            pltpu.make_async_copy(maps_hi.at[n], mh.at[n], msem.at[n, 0]),
            pltpu.make_async_copy(maps_lo.at[n], ml.at[n], msem.at[n, 1]),
        ]

    own = sc[BASE] // spots

    @pl.when(g == 0)
    def _():
        for s in range(steps):
            for n in range(4):
                if s == 0:
                    for c in bring_maps(n):
                        c.start()
                for side in range(2):
                    bring(s, 2 * n + side).start()

    parity = lax.rem(sc[CELL], 2)

    def layer_body(layer, _):
        partner = layer ^ own
        for side in range(2):
            n = 2 * partner + side
            pltpu.make_async_copy(blocks[0], buf.at[g, n], sem.at[g, n]).wait()

        @pl.when(g == 0)
        def _():
            for c in bring_maps(partner):
                c.wait()

        for side in range(2):
            start = pl.multiple_of(jnp.where(parity == side, 0, width), width)
            hi, lo = split(buf[g, 2 * partner + side, :spots, :])
            gh[:, pl.ds(start, width)] = hi
            gl[:, pl.ds(start, width)] = lo
        base = layer * spots
        low, low_end = slide_of(base, sc), slide_of(base + half - 1, sc)
        high, high_end = slide_of(base + half, sc), slide_of(base + spots - 1, sc)
        before = jnp.where(layer == 0, -1, slide_of(base - 1, sc))

        def put(k, value):
            res[k] = jnp.where(k > before, 0.0, res[k]) + value

        @pl.when(low == high_end)
        def _():
            put(low, mm3(mh[partner], ml[partner], gh[...], gl[...]))

        def slide_body(k, _):
            in_low, in_high = k <= low_end, k >= high

            def part(first, count):
                cols = pl.ds(first, count)
                ids = lax.broadcasted_iota(I32, (1, count), 1) + (base + first)
                keep = (slide_of(ids, sc) == k).astype(F32).astype(BF16)
                put(k, mm3(mh[partner, :, cols] * keep, ml[partner, :, cols] * keep, gh[cols, :], gl[cols, :]))

            @pl.when(in_low & in_high)
            def _():
                part(0, spots)

            @pl.when(jnp.logical_not(in_low & in_high))
            def _():
                part(pl.multiple_of(jnp.where(in_low, 0, half), half), half)

            return 0

        lax.fori_loop(low, jnp.where(low == high_end, low, high_end + 1), slide_body, 0)
        return 0

    lax.fori_loop(0, 4, layer_body, 0)
    slots = lax.broadcasted_iota(I32, (1, 4 * WINDOW), 1)

    def place_body(t, _):
        rows = block_rows(t, 128)
        for k in range(4):
            window = pl.ds(pl.multiple_of(table[t, k], 8), WINDOW)
            hi, lo = split(res[k, window, :])
            sh[k * WINDOW : (k + 1) * WINDOW, :] = hi
            sl[k * WINDOW : (k + 1) * WINDOW, :] = lo
        pick = (place[rows, :] == slots).astype(F32).astype(BF16)
        out[rows, :] = mm(pick, sh[...]) + mm(pick, sl[...])
        return 0

    lax.fori_loop(0, cells // 128, place_body, 0, unroll=4)


def expr_kernel(steps, layers, near, alias, sc, *refs):
    refs = list(refs)
    blocks = [refs.pop(0) for _ in range(2 * layers * steps)]
    maps = [(refs.pop(0), refs.pop(0)) for _ in range(layers)]
    acc = refs.pop(0) if near else None
    if alias:
        refs.pop(0)
    out, buf, sem = refs
    g = pl.program_id(0)
    cells, spots = maps[0][0].shape
    width = buf.shape[3]
    got = fetch(g, steps, blocks, buf, sem)
    parity = lax.rem(sc[CELL], 2)
    for side in range(2):
        start = pl.multiple_of(jnp.where(parity == side, 0, width), width)
        grads = [split(got[2 * n + side, :spots, :]) for n in range(layers)]

        def body(t, _):
            rows = block_rows(t, 256)
            value = None
            for (mh, ml), (gh, gl) in zip(maps, grads):
                term = mm3(mh[rows, :], ml[rows, :], gh, gl)
                value = term if value is None else value + term
            if acc is not None:
                value = acc[rows, pl.ds(start, width)] + value
            out[rows, pl.ds(start, width)] = value
            return 0

        lax.fori_loop(0, cells // 256, body, 0, unroll=True)


def tie(x, *others):
    return lax.optimization_barrier((x, *others))[0]


def whole(shape):
    return pl.BlockSpec(shape, lambda *_: (0,) * len(shape))


ANY = pl.BlockSpec(memory_space=pl.ANY)
HBM = pl.BlockSpec(memory_space=pltpu.HBM)
SMEM = pl.BlockSpec(memory_space=pltpu.SMEM)


def call(kernel, sc, args, in_specs, outs, out_specs, grid=(1,), scratch=(), flops=0, name=None, alias=None, size=None):
    if size is None:
        size = sum(x.size * x.dtype.itemsize for x in (*args, *jax.tree.leaves(outs)))
    return pl.pallas_call(
        kernel,
        out_shape=outs,
        grid_spec=pltpu.PrefetchScalarGridSpec(
            num_scalar_prefetch=len(sc), grid=grid, in_specs=in_specs, out_specs=out_specs, scratch_shapes=scratch
        ),
        cost_estimate=pl.CostEstimate(flops=flops, bytes_accessed=size, transcendentals=0),
        input_output_aliases=alias or {},
        name=name,
    )(*sc, *args)


def fast(logits, expression, spatial, spot_counts, cell_mask, cell_slide):
    cells, spots = logits.shape
    genes = expression.shape[1]
    n_cell, n_spot = lax.axis_size("cell"), lax.axis_size("spot")
    width = genes // n_cell
    half, rows = spots // 2, spots + EXTRA
    ci, zi = lax.axis_index("cell"), lax.axis_index("spot")
    places = [ci, *((zi ^ k) * spots for k in range(n_spot))]
    sc = (jnp.concatenate([spot_counts, jnp.stack(places), jnp.array(BLOCKS, I32)]).astype(I32),)
    sds = jax.ShapeDtypeStruct
    block_sds, block_spec = sds((rows, width), F32), whole((rows, width))

    put_scratch = [pltpu.VMEM((2, rows, width), F32), pltpu.SemaphoreType.DMA((2,))]

    def cell_swap(x, bit):
        return lax.ppermute(x, "cell", [(i, i ^ bit) for i in range(n_cell)])

    def spot_swap(x, k):
        return lax.ppermute(x, "spot", [(i, i ^ k) for i in range(n_spot)])

    def spot_move(x, moves):
        return lax.ppermute(x, "spot", moves)

    def genes_spec(first):
        return pl.BlockSpec((cells, width), lambda g, sc, *_: (0, sc[CELL] ^ sc[ORDER + first + g]))

    hi, lo, eth, etl, compact, extra, place, table, b7, b6 = call(
        first_kernel, sc, (logits, cell_mask.reshape(-1, 128), cell_slide.reshape(-1, 128), expression),
        [whole((cells, spots)), whole((cells // 128, 128)), whole((cells // 128, 128)), genes_spec(0)],
        (
            sds((cells, spots), BF16), sds((cells, spots), BF16), sds((spots, cells), BF16), sds((spots, cells), BF16),
            sds((CAPACITY, spots), F32), sds((EXTRA, width), F32), sds((cells, 1), I32), sds((cells // 128, 128), I32),
            block_sds, block_sds,
        ),
        (
            HBM, HBM, HBM, HBM, whole((CAPACITY, spots)), whole((EXTRA, width)), whole((cells, 1)), whole((cells // 128, 128)), ANY, ANY,
        ),
        grid=(2,), scratch=[
            pltpu.VMEM((CAPACITY, cells), BF16), *put_scratch, pltpu.VMEM((cells, spots), BF16), pltpu.VMEM((cells, spots), BF16),
            pltpu.VMEM((spots, cells), BF16), pltpu.VMEM((spots, cells), BF16), pltpu.SemaphoreType.DMA((4,)),
        ],
        flops=4 * cells * spots * CAPACITY + 12 * cells * spots * width, name="first",
    )

    def products(first, parts, extra, size=None):
        count = sum(parts)
        return call(
            more_kernel, sc, (eth, etl, expression, extra),
            [whole((spots, cells)), whole((spots, cells)), genes_spec(first), whole((EXTRA, width))],
            tuple(sds((n, rows, width), F32) for n in parts), (ANY,) * len(parts), scratch=put_scratch,
            grid=(count,), flops=0 if size == 0 else 6 * cells * spots * width * count, name="more", size=size,
        )

    far_m, far1 = spot_move(compact, MIDDLE), spot_swap(compact, 1)
    top3, low3 = call(
        diagonal_kernel, sc, (b6, cell_swap(b7, 1)), [HBM] * 2,
        (sds((half, width), F32), sds((rows - half, width), F32)),
        (whole((half, width)), whole((rows - half, width))), name="diagonal", size=0,
        scratch=[pltpu.VMEM((rows, width), F32), pltpu.VMEM((rows, width), F32), pltpu.SemaphoreType.DMA((4,))],
    )
    in_top, in_low = cell_swap(top3, 2), cell_swap(low3, 4)
    (odd,) = products(2, (3,), tie(extra, top3), 0)
    far_n, far_e = spot_move(tie(far1, far_m, odd), MIDDLE), spot_move(tie(far_m, far1, odd), OUTWARD)
    in_odd = cell_swap(tie(odd, far1, far_m, in_top, in_low), 1)
    (even,) = products(5, (3,), tie(extra, odd, far1, far_m))
    one, two = call(
        merge_kernel, sc, (even, in_odd, in_low, in_top),
        [HBM] * 4, (block_sds, block_sds), (block_spec, block_spec), name="merge",
        scratch=[
            pltpu.VMEM((2, rows, width), F32), pltpu.VMEM((2, rows, width), F32), pltpu.VMEM((rows - half, width), F32),
            pltpu.VMEM((half, width), F32), pltpu.SemaphoreType.DMA((6,)),
        ],
    )
    in_x, in_y = cell_swap(one, 2), cell_swap(two, 4)
    far_f = spot_move(tie(far_n, far_e, one), OUTWARD)
    own_spatial = pl.BlockSpec((spots, width), lambda g, sc, *_: (0, sc[CELL]))
    small = whole((16, width))
    one_block = pl.BlockSpec((None, rows, width), lambda *_: (2, 0, 0))
    predicted, sums, extra_all, over = call(
        sums_kernel, sc, (even, in_odd, in_x, in_y, spatial),
        [one_block, one_block, block_spec, block_spec, own_spatial],
        (sds((spots, width), F32), sds((16, width), F32), sds((EXTRA, width), F32), sds((1,), F32)),
        (whole((spots, width)), small, whole((EXTRA, width)), SMEM), flops=5 * 10**9, name="sums",
    )
    all_sums = [sums, *(spot_swap(tie(sums, far_f), k) for k in range(1, n_spot))]
    maps_shape = (n_spot, CAPACITY, spots)
    comps = call(
        halves_kernel, sc, (tie(compact, sums), far1, far_n, far_e, far_m, far_f), [whole((CAPACITY, spots))] * 6,
        (sds(maps_shape, BF16),) * 2, (whole(maps_shape),) * 2, name="halves",
    )
    block, cosines = call(
        grad_kernel, sc, (tie(predicted, comps[0]), spatial, extra_all, *all_sums),
        [whole((spots, width)), own_spatial, whole((EXTRA, width))] + [small] * n_spot,
        (block_sds, sds((4, width), F32)), (block_spec, whole((4, width))), name="grad",
    )

    def pair(g, sc, qs):
        q = qs[0]
        for n, value in enumerate(qs):
            q = jnp.where(g == n, value, q) if n else q
        return (sc[CELL] // 2) ^ q

    def logit_part(got, qs, sums=None):
        blocks = [x for q in qs for x in got[q]]
        sizes = ((cells, spots), (EXTRA, width), (n_cell, EXTRA, 128))
        args = [expression, *blocks]
        specs = [
            pl.BlockSpec((cells, 2 * width), lambda g, sc, *_: (0, pair(g, sc, qs))), *[ANY] * len(blocks),
        ]
        outs, scratch = sizes, []
        if sums is not None:
            args += [hi, lo, *sums]
            specs += [whole((cells, spots)), whole((cells, spots)), *map(whole, sizes)]
            outs, scratch = ((cells, spots), (4,)), [pltpu.VMEM(size, F32) for size in sizes]
        steps = len(qs)
        return call(
            functools.partial(logit_kernel, steps, qs), sc, args, specs,
            tuple(sds(size, F32) for size in outs), tuple(whole(o) if len(o) > 1 else SMEM for o in outs), grid=(steps,),
            scratch=[*scratch, pltpu.VMEM((steps, 2, rows, width), F32), pltpu.SemaphoreType.DMA((steps, 2))],
            flops=12 * cells * spots * width * steps, name="logit",
        )

    def rows_part(gots, comps, qs, onto=None, space=ANY):
        blocks = [x for q in qs for got in gots for x in got[q]]
        args = [*blocks, *comps, place]
        specs = [space] * (len(blocks) + 2) + [whole((cells, 1))]
        alias = None
        if onto is not None:
            alias = {len(args) + 2: 0}
            args.append(onto)
            specs.append(ANY)
        steps = len(qs)
        return call(
            functools.partial(rows_kernel, steps, int(onto is not None)), (*sc, table), args, specs,
            sds((cells, genes), F32), pl.BlockSpec((cells, 2 * width), lambda g, sc, *_: (0, pair(g, sc, qs))),
            grid=(steps,), alias=alias,
            scratch=[
                pltpu.VMEM((steps, 8, rows, width), F32), pltpu.SemaphoreType.DMA((steps, 8)),
                pltpu.VMEM((4, CAPACITY, spots), BF16), pltpu.VMEM((4, CAPACITY, spots), BF16),
                pltpu.SemaphoreType.DMA((4, 2)),
                pltpu.VMEM((spots, 2 * width), BF16), pltpu.VMEM((spots, 2 * width), BF16),
                pltpu.VMEM((4, CAPACITY, 2 * width), F32),
                pltpu.VMEM((4 * WINDOW, 2 * width), BF16), pltpu.VMEM((4 * WINDOW, 2 * width), BF16),
            ],
            name="rows",
        )

    def expr_part(gots, maps, qs, near=None, final=False, onto=None):
        blocks = [x for q in qs for got in gots for x in got[q]]
        args = [*blocks, *(m for pairs in maps for m in pairs)]
        specs = [ANY] * len(blocks) + [whole((cells, spots))] * (2 * len(maps))
        columns = pl.BlockSpec((cells, 2 * width), lambda g, sc, *_: (0, pair(g, sc, qs)))
        steps_spec = pl.BlockSpec((None, cells, 2 * width), lambda g, sc, *_: (g, 0, 0))
        alias = None
        if near is not None:
            args.append(near)
            specs.append(steps_spec)
        if onto is not None:
            alias = {len(args) + 1: 0}
            args.append(onto)
            specs.append(ANY)
        out = sds((cells, genes) if final else (len(qs), cells, 2 * width), F32)
        scratch = [
            pltpu.VMEM((len(qs), 2 * len(maps), rows, width), F32),
            pltpu.SemaphoreType.DMA((len(qs), 2 * len(maps))),
        ]
        return call(
            functools.partial(expr_kernel, len(qs), len(maps), near is not None, onto is not None), sc, args, specs,
            out, columns if final else steps_spec, grid=(len(qs),), scratch=scratch, alias=alias,
            flops=6 * cells * spots * 2 * width * len(qs) * len(maps), name="expr",
        )

    def cores(x, *others):
        return (x, cell_swap(tie(x, *others) if others else x, 1))

    o_x, o_y = cell_swap(block, 2), cell_swap(block, 4)
    z1, mid = spot_swap(block, 1), spot_move(block, MIDDLE)
    got_o = {0: cores(block), 1: cores(o_x)}
    a_x, o_d = cell_swap(tie(z1, o_x), 2), cell_swap(tie(o_x, o_y, z1), 4)
    mid2, end2 = spot_move(tie(z1, mid), MIDDLE), spot_move(tie(mid, z1), OUTWARD)
    part = logit_part(got_o, (0, 1))
    z2 = tie(mid2, part[0]) + end2
    a_y = cell_swap(tie(z1, o_d, part[0]), 4)
    c_x = cell_swap(tie(z2, a_x, part[0]), 2)
    end3 = spot_move(tie(mid2, end2, part[0]), OUTWARD)
    got_o[2], got_o[3] = cores(o_y, part[0], a_x, z2), cores(o_d, part[0], a_x, z2)
    logit_grad, losses = logit_part(got_o, (2, 3), part)
    z3 = tie(mid, logit_grad) + end3
    c_y = cell_swap(tie(z2, a_y, logit_grad), 4)
    d_x = cell_swap(tie(z3, c_x, logit_grad), 2)
    early = (got_o[2][1], got_o[3][1])
    got_a, got_c = {0: cores(z1, *early)}, {0: cores(z2, *early)}
    got_d = {0: cores(z3, got_a[0][1], got_c[0][1], a_y, c_x)}
    gots = (got_o, got_a, got_c, got_d)
    body = rows_part(gots, comps, (0,))
    a_d, d_y = cell_swap(tie(a_y, d_x, body), 2), cell_swap(tie(z3, c_y, body), 4)
    early = (logit_grad, got_d[0][1])
    got_a[1], got_c[1] = cores(a_x, *early), cores(c_x, *early)
    got_d[1] = cores(d_x, got_a[1][1], got_c[1][1], body, c_y)
    body = rows_part(gots, comps, (1,), body)
    d_d, c_d = cell_swap(tie(d_y, a_d, body), 2), cell_swap(tie(c_x, d_y, body), 4)
    got_a[2], got_c[2] = cores(a_y, got_d[1][1]), cores(c_y, got_d[1][1])
    got_d[2] = cores(d_y, got_a[2][1], got_c[2][1], a_d, body)
    got_a[3] = cores(a_d, body, got_d[2][1])
    body = rows_part(gots, comps, (2,), body)
    got_c[3], got_d[3] = cores(c_d, body, got_a[3][1]), cores(d_d, body, got_a[3][1])

    def direct(operands):
        body, last = operands[:2]
        return rows_part(last, comps, (3,), body, HBM)

    def exchange(operands):
        term = expr_part((operands[2],), ((hi, lo),), (0, 1, 2, 3), final=True)
        one, two, three = (spot_swap(term, k) for k in (1, 2, 3))
        return (term + one) + (two + three)

    expression_grad = lax.cond(
        over[0] > 0, exchange, direct, (body, [{3: got[3]} for got in gots], got_o)
    )

    return losses, predicted, cosines, logit_grad, expression_grad


def plain(logits, expression, spatial, spot_counts, cell_mask, cell_slide):
    spot_cols = logits.shape[1]
    gene_total = expression.shape[1]
    slide_total = spot_counts.shape[0]
    gene_rows = gene_total // lax.axis_size("cell")
    gene_start = lax.axis_index("cell") * gene_rows
    slide_ends = jnp.cumsum(spot_counts)
    spot_ids = lax.axis_index("spot") * spot_cols + jnp.arange(spot_cols, dtype=I32)
    spot_slide = jnp.sum((spot_ids[:, None] >= slide_ends[None, : slide_total - 1]).astype(I32), axis=1)
    member = (cell_mask[:, None] == 1) & (cell_slide[:, None] == spot_slide[None, :])
    onehot = (spot_slide[:, None] == jnp.arange(slide_total, dtype=I32)[None, :]).astype(F32)
    exponent = jnp.where(member, jnp.exp(logits), 0.0)
    column_total = lax.psum(jnp.sum(exponent, axis=0), "cell")
    mapping = exponent / column_total[None, :]
    predicted = lax.psum_scatter(
        lax.dot_general(expression, mapping, (((0,), (0,)), ((), ())), precision=HIGH),
        "cell", scatter_dimension=0, tiled=True,
    ).T
    spatial_own = lax.dynamic_slice_in_dim(spatial, gene_start, gene_rows, 1)
    sum_a, sum_b, sum_c = lax.psum(
        tuple(
            jnp.dot(onehot.T, t, precision=HIGH)
            for t in (predicted * spatial_own, predicted * predicted, spatial_own * spatial_own)
        ),
        "spot",
    )
    inverse_norms = lax.rsqrt(sum_b) * lax.rsqrt(sum_c)
    cosines = sum_a * inverse_norms
    spread_inv = jnp.dot(onehot, inverse_norms, precision=HIGH)
    spread_cos = jnp.dot(onehot, cosines / sum_b, precision=HIGH)
    pred_grad = -(spatial_own * spread_inv - predicted * spread_cos)
    losses, column_dot = lax.psum((-jnp.sum(cosines, axis=1), jnp.sum(predicted * pred_grad, axis=1)), "cell")
    grad_full = lax.all_gather(pred_grad, "cell", axis=1, tiled=True)
    map_grad = lax.dot_general(expression, grad_full, (((1,), (1,)), ((), ())), precision=HIGH)
    logit_grad = mapping * (map_grad - column_dot[None, :])
    expression_grad = lax.psum(jnp.dot(mapping, grad_full, precision=HIGH), "spot")
    return losses, predicted, cosines, logit_grad, expression_grad


def solution(mesh):
    small = mesh.shape["cell"] == 8 and mesh.shape["spot"] == 4
    return jax.shard_map(
        fast if small else plain,
        mesh=mesh,
        in_specs=(P("cell", "spot"), P("cell", None), P("spot", None), P(), P("cell"), P("cell")),
        out_specs=(P(), P("spot", "cell"), P(None, "cell"), P("cell", "spot"), P("cell", None)),
        check_vma=False,
    )
```

```python
import functools

import jax
import jax.numpy as jnp
from jax import lax
from jax.experimental import pallas as pl
from jax.experimental.pallas import tpu as pltpu
from jax.sharding import PartitionSpec as P

HIGH = lax.Precision.HIGHEST
F32, BF16, I32 = jnp.float32, jnp.bfloat16, jnp.int32
CAPACITY = 304
EXTRA = 8
WINDOW = 64
MIDDLE = ((1, 2), (2, 1))
OUTWARD = ((1, 0), (2, 3))
COUNTS, CELL, BASE, ORDER = 0, 4, 5, 9
BLOCKS = (7, 6, 3, 5, 1, 2, 4, 0)


def split(x):
    hi = x.astype(BF16)
    return hi, (x - hi.astype(F32)).astype(BF16)


def mm(a, b, dims=((1,), (0,))):
    return lax.dot_general(a, b, (dims, ((), ())), preferred_element_type=F32)


def mm3(ah, al, bh, bl, dims=((1,), (0,))):
    return mm(ah, bh, dims) + (mm(ah, bl, dims) + mm(al, bh, dims))


def slide_of(ids, sc):
    end, slide = 0, 0
    for k in range(3):
        end = end + sc[COUNTS + k]
        slide = slide + (ids >= end).astype(I32)
    return slide


def block_rows(t, step):
    return pl.ds(pl.multiple_of(t * step, step), step)


def first_kernel(sc, logits, mask, slide, expr, *refs):
    *kept, compact_out, extra_out, place_out, table_out = refs[:8]
    *outs, rbuf, obuf, sem, hi_out, lo_out, eth, etl, ksem = refs[8:]
    cells, spots = logits.shape
    cap, width = compact_out.shape[0], extra_out.shape[1]
    step = 128
    g = pl.program_id(0)

    @pl.when(g == 0)
    def _():
        lane = lax.broadcasted_iota(I32, (1, spots), 1) + sc[BASE]
        spot_slide = slide_of(lane, sc)
        lanes = lax.broadcasted_iota(I32, (1, step), 1).astype(F32)
        lower = (
            lax.broadcasted_iota(I32, (step, step), 0) > lax.broadcasted_iota(I32, (step, step), 1)
        ).astype(BF16)

        def body(t, carry):
            total, seen, widest = carry
            rows = block_rows(t, step)
            one = pl.ds(t, 1)
            own_row = jnp.where(mask[one, :] == 1, slide[one, :], -1).astype(F32)
            own = jnp.broadcast_to(own_row, (step, step)).T[:, :1]
            e = jnp.where(own.astype(I32) == spot_slide, jnp.exp(logits[rows, :]), 0.0)
            hi, lo = split(e)
            e = hi.astype(F32) + lo.astype(F32)
            hi, lo = split(e)
            hi_out[rows, :] = hi
            lo_out[rows, :] = lo
            hit, lit = split(e.T)
            eth[:, rows] = hit
            etl[:, rows] = lit
            onehot = (own == lanes).astype(F32)
            before = mm(lower, onehot.astype(BF16)) + seen
            rank = jnp.sum(onehot * before, axis=1, keepdims=True)
            rank = jnp.where(own >= 0, rank, -1.0)
            window = jnp.minimum((seen.astype(I32) // 8) * 8, cap - WINDOW)
            table_out[one, :] = window
            window = window.astype(F32)
            local = jnp.sum(onehot * (before - window), axis=1, keepdims=True) + WINDOW * own
            place_out[rows, :] = jnp.where(own >= 0, local, -1.0).astype(I32)
            row = jnp.broadcast_to(rank, (step, step)).T[:1, :].astype(I32)
            rbuf[:, rows] = (lax.broadcasted_iota(I32, (cap, step), 0) == row).astype(F32).astype(BF16)
            after = seen + jnp.sum(onehot, axis=0, keepdims=True)
            return total + jnp.sum(e, axis=0, keepdims=True), after, jnp.maximum(widest, after - window)

        zero = jnp.zeros((1, step), F32)
        total, seen, widest = lax.fori_loop(
            0, cells // step, body, (jnp.zeros((1, spots), F32), zero, zero), unroll=2
        )
        compact_out[...] = mm(rbuf[...], hi_out[...]) + mm(rbuf[...], lo_out[...])
        extra_out[...] = jnp.zeros_like(extra_out)
        for h in range(spots // width):
            extra_out[h : h + 1, :] = total[:, h * width : (h + 1) * width]
        over = jnp.maximum((seen > cap).astype(F32), (widest > WINDOW).astype(F32))
        over = jnp.max(over, axis=1, keepdims=True)
        extra_out[EXTRA - 1 : EXTRA, :] = jnp.broadcast_to(over, (1, width))
        load(list(zip((hi_out, lo_out, eth, etl), kept)), ksem)

    product(g, eth, etl, expr, extra_out, outs, obuf, sem)

    @pl.when(g == 1)
    def _():
        for n, (source, place) in enumerate(zip((hi_out, lo_out, eth, etl), kept)):
            pltpu.make_async_copy(source, place, ksem.at[n]).wait()


def product(g, eth, etl, expr, extra, outs, obuf, sem):
    spots = eth.shape[0]
    count = len(outs)
    slot = lax.rem(g, 2)

    def put(n):
        return pltpu.make_async_copy(obuf.at[n % 2], outs[n], sem.at[n % 2])

    for n in range(2, count):

        @pl.when(g == n)
        def _():
            put(n - 2).wait()

    xh, xl = split(expr[...])
    obuf[slot, :spots, :] = mm3(eth[...], etl[...], xh, xl)
    obuf[slot, spots:, :] = extra[...]
    for n in range(count):

        @pl.when(g == n)
        def _():
            put(n).start()

    @pl.when(g == count - 1)
    def _():
        for n in range(count - 2, count):
            put(n).wait()


def more_kernel(sc, eth, etl, expr, extra, *refs):
    *outs, obuf, sem = refs
    views = [out.at[n] for out in outs for n in range(out.shape[0])]
    product(pl.program_id(0), eth, etl, expr, extra, views, obuf, sem)


def load(pairs, sem):
    copies = [pltpu.make_async_copy(source, place, sem.at[n]) for n, (source, place) in enumerate(pairs)]
    for c in copies:
        c.start()
    return copies


def diagonal_kernel(sc, a, b, top, bottom, abuf, bbuf, sem):
    half = top.shape[0]
    upper, lower = pl.ds(0, half), pl.ds(half, bottom.shape[0])
    parts = [(x.at[r], y.at[r]) for r in (upper, lower) for x, y in ((a, abuf), (b, bbuf))]
    copies = load(parts, sem)
    for c in copies[:2]:
        c.wait()
    top[...] = abuf[upper, :] + bbuf[upper, :]
    for c in copies[2:]:
        c.wait()
    bottom[...] = abuf[lower, :] + bbuf[lower, :]


def merge_kernel(sc, a, b, low, high, one, two, abuf, bbuf, lbuf, hbuf, sem):
    half = high.shape[0]
    copies = load(
        [(a.at[0], abuf.at[0]), (b.at[0], bbuf.at[0]), (low, lbuf), (a.at[1], abuf.at[1]), (b.at[1], bbuf.at[1]), (high, hbuf)],
        sem,
    )
    for c in copies[:3]:
        c.wait()
    one[:half, :] = abuf[0, :half, :] + bbuf[0, :half, :]
    one[half:, :] = (abuf[0, half:, :] + bbuf[0, half:, :]) + lbuf[...]
    for c in copies[3:]:
        c.wait()
    two[:half, :] = (abuf[1, :half, :] + bbuf[1, :half, :]) + hbuf[...]
    two[half:, :] = abuf[1, half:, :] + bbuf[1, half:, :]


def totals(extra_rows, spots):
    width = extra_rows.shape[1]
    cols = [
        jnp.broadcast_to(extra_rows[h : h + 1, :], (128, width)).T[:, :1] for h in range(spots // width)
    ]
    return jnp.concatenate(cols, axis=0)


def sums_kernel(sc, a, b, x, y, spatial, pred_out, sums_out, extra_out, over_out):
    spots = pred_out.shape[0]
    extra = (a[spots:, :] + b[spots:, :]) + (x[spots:, :] + y[spots:, :])
    extra_out[...] = extra
    over_out[0] = extra[EXTRA - 1, 0]
    z = totals(extra, spots)
    pred = ((a[:spots, :] + b[:spots, :]) + (x[:spots, :] + y[:spots, :])) / z
    pred_out[...] = pred
    spat = spatial[...]
    ids = lax.broadcasted_iota(I32, (spots, 1), 0) + sc[BASE]
    slide = slide_of(ids, sc)
    sums_out[...] = jnp.zeros_like(sums_out)
    for n, term in enumerate((pred * spat, pred * pred, spat * spat)):
        for k in range(4):
            sums_out[4 * n + k : 4 * n + k + 1, :] = jnp.sum(
                jnp.where(slide == k, term, 0.0), axis=0, keepdims=True
            )


def grad_kernel(sc, pred, spatial, extra, s0, s1, s2, s3, blk_out, cos_out):
    spots, width = pred.shape
    sums = (s0[...] + s1[...]) + (s2[...] + s3[...])
    a, b, c = sums[0:4, :], sums[4:8, :], sums[8:12, :]
    inv = lax.rsqrt(b) * lax.rsqrt(c)
    cos = a * inv
    ratio = cos / b
    cos_out[...] = cos
    ids = lax.broadcasted_iota(I32, (spots, 1), 0) + sc[BASE]
    slide = slide_of(ids, sc)
    spread_inv, spread_cos = inv[3:4, :], ratio[3:4, :]
    for k in range(3):
        spread_inv = jnp.where(slide == k, inv[k : k + 1, :], spread_inv)
        spread_cos = jnp.where(slide == k, ratio[k : k + 1, :], spread_cos)
    p = pred[...]
    grad = -(spatial[...] * spread_inv - p * spread_cos) / totals(extra[...], spots)
    blk_out[:spots, :] = grad
    dots = lax.dot_general(
        jnp.ones((8, width), F32), p * grad, (((1,), (1,)), ((), ())),
        precision=HIGH, preferred_element_type=F32,
    )
    blk_out[spots:, :] = jnp.zeros((EXTRA, width), F32)
    for h in range(spots // width):
        blk_out[spots + h : spots + h + 1, :] = dots[:1, h * width : (h + 1) * width]
    blk_out[spots + 4 : spots + 8, :] = cos


def fetch(g, steps, blocks, buf, sem):
    per = len(blocks) // steps

    def copies(s):
        return [pltpu.make_async_copy(blocks[s * per + n], buf.at[s, n], sem.at[s, n]) for n in range(per)]

    @pl.when(g == 0)
    def _():
        for s in range(steps):
            for c in copies(s):
                c.start()

    for s in range(steps):

        @pl.when(g == s)
        def _():
            for c in copies(s):
                c.wait()

    return buf.at[g]


def logit_kernel(steps, qs, sc, expr, *refs):
    blocks, refs = refs[: 2 * steps], refs[2 * steps :]
    final = qs[0] > 0
    if final:
        hi, lo, acc_in, dots_in, parts_in, out, loss_out, acc, dots, parts, buf, sem = refs
    else:
        acc, dots, parts, buf, sem = refs
    g = pl.program_id(0)
    cells, spots = acc.shape
    width = buf.shape[3]
    got = fetch(g, steps, blocks, buf, sem)

    @pl.when(g == 0)
    def _():
        dots[...] = dots_in[...] if final else jnp.zeros_like(dots)
        if final:
            parts[...] = parts_in[...]
        else:
            parts[...] = jnp.zeros_like(parts)

    parity = lax.rem(sc[CELL], 2)

    def add(first):
        halves = []
        for side in range(2):
            start = pl.multiple_of(jnp.where(parity == side, 0, width), width)
            gh, gl = split(got[side, :spots, :])
            dots[...] += got[side, spots:, :]
            sums = jnp.sum(got[side, spots:, :], axis=1, keepdims=True)
            parts[sc[CELL] ^ (2 * (g + qs[0]) + side)] = jnp.broadcast_to(sums, parts.shape[1:])
            halves.append((start, gh, gl))

        def body(t, _):
            rows = block_rows(t, 256)
            value = None
            for start, gh, gl in halves:
                xh, xl = split(expr[rows, pl.ds(start, width)])
                term = mm3(xh, xl, gh, gl, ((1,), (1,)))
                value = term if value is None else value + term
            if not first:
                acc[rows, :] += value
            elif final:
                acc[rows, :] = acc_in[rows, :] + value
            else:
                acc[rows, :] = value
            return 0

        lax.fori_loop(0, cells // 256, body, 0, unroll=True)

    @pl.when(g == 0)
    def _():
        add(True)

    @pl.when(g > 0)
    def _():
        add(False)

    if final:

        @pl.when(g == steps - 1)
        def _():
            row = jnp.concatenate([dots[h : h + 1, :] for h in range(spots // width)], axis=1)
            e = hi[...].astype(F32) + lo[...].astype(F32)
            out[...] = e * (acc[...] - row)
            total = parts[0]
            for n in range(1, parts.shape[0]):
                total = total + parts[n]
            for k in range(4):
                loss_out[k] = -total[4 + k, 0]


def halves_kernel(sc, compact, far1, far_n, far_e, far_m, far_f, hi_out, lo_out):
    spots = compact.shape[1]
    middle = (sc[BASE] == spots) | (sc[BASE] == 2 * spots)
    two = jnp.where(middle, far_n[...], far_e[...])
    three = jnp.where(middle, far_m[...], far_f[...])
    for n, value in enumerate((compact[...], far1[...], two, three)):
        hi_out[n], lo_out[n] = split(value)


def rows_kernel(steps, alias, sc, table, *refs):
    blocks, refs = refs[: 8 * steps], refs[8 * steps :]
    (maps_hi, maps_lo, place), refs = refs[:3], refs[3 + alias :]
    out, buf, sem, mh, ml, msem, gh, gl, res, sh, sl = refs
    g = pl.program_id(0)
    cells = out.shape[0]
    cap, spots = mh.shape[1:]
    width = buf.shape[3]
    half = spots // 2

    def bring(s, n):
        return pltpu.make_async_copy(blocks[8 * s + n], buf.at[s, n], sem.at[s, n])

    def bring_maps(n):
        return [
            pltpu.make_async_copy(maps_hi.at[n], mh.at[n], msem.at[n, 0]),
            pltpu.make_async_copy(maps_lo.at[n], ml.at[n], msem.at[n, 1]),
        ]

    own = sc[BASE] // spots

    @pl.when(g == 0)
    def _():
        for s in range(steps):
            for n in range(4):
                if s == 0:
                    for c in bring_maps(n):
                        c.start()
                for side in range(2):
                    bring(s, 2 * n + side).start()

    parity = lax.rem(sc[CELL], 2)

    def layer_body(layer, _):
        partner = layer ^ own
        for side in range(2):
            n = 2 * partner + side
            pltpu.make_async_copy(blocks[0], buf.at[g, n], sem.at[g, n]).wait()

        @pl.when(g == 0)
        def _():
            for c in bring_maps(partner):
                c.wait()

        for side in range(2):
            start = pl.multiple_of(jnp.where(parity == side, 0, width), width)
            hi, lo = split(buf[g, 2 * partner + side, :spots, :])
            gh[:, pl.ds(start, width)] = hi
            gl[:, pl.ds(start, width)] = lo
        base = layer * spots
        low, low_end = slide_of(base, sc), slide_of(base + half - 1, sc)
        high, high_end = slide_of(base + half, sc), slide_of(base + spots - 1, sc)
        before = jnp.where(layer == 0, -1, slide_of(base - 1, sc))

        def put(k, value):
            res[k] = jnp.where(k > before, 0.0, res[k]) + value

        @pl.when(low == high_end)
        def _():
            put(low, mm3(mh[partner], ml[partner], gh[...], gl[...]))

        def slide_body(k, _):
            in_low, in_high = k <= low_end, k >= high

            def part(first, count):
                cols = pl.ds(first, count)
                ids = lax.broadcasted_iota(I32, (1, count), 1) + (base + first)
                keep = (slide_of(ids, sc) == k).astype(F32).astype(BF16)
                put(k, mm3(mh[partner, :, cols] * keep, ml[partner, :, cols] * keep, gh[cols, :], gl[cols, :]))

            @pl.when(in_low & in_high)
            def _():
                part(0, spots)

            @pl.when(jnp.logical_not(in_low & in_high))
            def _():
                part(pl.multiple_of(jnp.where(in_low, 0, half), half), half)

            return 0

        lax.fori_loop(low, jnp.where(low == high_end, low, high_end + 1), slide_body, 0)
        return 0

    lax.fori_loop(0, 4, layer_body, 0)
    slots = lax.broadcasted_iota(I32, (1, 4 * WINDOW), 1)

    def place_body(t, _):
        rows = block_rows(t, 128)
        for k in range(4):
            window = pl.ds(pl.multiple_of(table[t, k], 8), WINDOW)
            hi, lo = split(res[k, window, :])
            sh[k * WINDOW : (k + 1) * WINDOW, :] = hi
            sl[k * WINDOW : (k + 1) * WINDOW, :] = lo
        pick = (place[rows, :] == slots).astype(F32).astype(BF16)
        out[rows, :] = mm(pick, sh[...]) + mm(pick, sl[...])
        return 0

    lax.fori_loop(0, cells // 128, place_body, 0, unroll=8)


def expr_kernel(steps, layers, near, alias, sc, *refs):
    refs = list(refs)
    blocks = [refs.pop(0) for _ in range(2 * layers * steps)]
    maps = [(refs.pop(0), refs.pop(0)) for _ in range(layers)]
    acc = refs.pop(0) if near else None
    if alias:
        refs.pop(0)
    out, buf, sem = refs
    g = pl.program_id(0)
    cells, spots = maps[0][0].shape
    width = buf.shape[3]
    got = fetch(g, steps, blocks, buf, sem)
    parity = lax.rem(sc[CELL], 2)
    for side in range(2):
        start = pl.multiple_of(jnp.where(parity == side, 0, width), width)
        grads = [split(got[2 * n + side, :spots, :]) for n in range(layers)]

        def body(t, _):
            rows = block_rows(t, 256)
            value = None
            for (mh, ml), (gh, gl) in zip(maps, grads):
                term = mm3(mh[rows, :], ml[rows, :], gh, gl)
                value = term if value is None else value + term
            if acc is not None:
                value = acc[rows, pl.ds(start, width)] + value
            out[rows, pl.ds(start, width)] = value
            return 0

        lax.fori_loop(0, cells // 256, body, 0, unroll=True)


def tie(x, *others):
    return lax.optimization_barrier((x, *others))[0]


def whole(shape):
    return pl.BlockSpec(shape, lambda *_: (0,) * len(shape))


ANY = pl.BlockSpec(memory_space=pl.ANY)
HBM = pl.BlockSpec(memory_space=pltpu.HBM)
SMEM = pl.BlockSpec(memory_space=pltpu.SMEM)


def call(kernel, sc, args, in_specs, outs, out_specs, grid=(1,), scratch=(), flops=0, name=None, alias=None, size=None):
    if size is None:
        size = sum(x.size * x.dtype.itemsize for x in (*args, *jax.tree.leaves(outs)))
    return pl.pallas_call(
        kernel,
        out_shape=outs,
        grid_spec=pltpu.PrefetchScalarGridSpec(
            num_scalar_prefetch=len(sc), grid=grid, in_specs=in_specs, out_specs=out_specs, scratch_shapes=scratch
        ),
        cost_estimate=pl.CostEstimate(flops=flops, bytes_accessed=size, transcendentals=0),
        input_output_aliases=alias or {},
        name=name,
    )(*sc, *args)


def fast(logits, expression, spatial, spot_counts, cell_mask, cell_slide):
    cells, spots = logits.shape
    genes = expression.shape[1]
    n_cell, n_spot = lax.axis_size("cell"), lax.axis_size("spot")
    width = genes // n_cell
    half, rows = spots // 2, spots + EXTRA
    ci, zi = lax.axis_index("cell"), lax.axis_index("spot")
    places = [ci, *((zi ^ k) * spots for k in range(n_spot))]
    sc = (jnp.concatenate([spot_counts, jnp.stack(places), jnp.array(BLOCKS, I32)]).astype(I32),)
    sds = jax.ShapeDtypeStruct
    block_sds, block_spec = sds((rows, width), F32), whole((rows, width))

    put_scratch = [pltpu.VMEM((2, rows, width), F32), pltpu.SemaphoreType.DMA((2,))]

    def cell_swap(x, bit):
        return lax.ppermute(x, "cell", [(i, i ^ bit) for i in range(n_cell)])

    def spot_swap(x, k):
        return lax.ppermute(x, "spot", [(i, i ^ k) for i in range(n_spot)])

    def spot_move(x, moves):
        return lax.ppermute(x, "spot", moves)

    def genes_spec(first):
        return pl.BlockSpec((cells, width), lambda g, sc, *_: (0, sc[CELL] ^ sc[ORDER + first + g]))

    hi, lo, eth, etl, compact, extra, place, table, b7, b6 = call(
        first_kernel, sc, (logits, cell_mask.reshape(-1, 128), cell_slide.reshape(-1, 128), expression),
        [whole((cells, spots)), whole((cells // 128, 128)), whole((cells // 128, 128)), genes_spec(0)],
        (
            sds((cells, spots), BF16), sds((cells, spots), BF16), sds((spots, cells), BF16), sds((spots, cells), BF16),
            sds((CAPACITY, spots), F32), sds((EXTRA, width), F32), sds((cells, 1), I32), sds((cells // 128, 128), I32),
            block_sds, block_sds,
        ),
        (
            HBM, HBM, HBM, HBM, whole((CAPACITY, spots)), whole((EXTRA, width)), whole((cells, 1)), whole((cells // 128, 128)), ANY, ANY,
        ),
        grid=(2,), scratch=[
            pltpu.VMEM((CAPACITY, cells), BF16), *put_scratch, pltpu.VMEM((cells, spots), BF16), pltpu.VMEM((cells, spots), BF16),
            pltpu.VMEM((spots, cells), BF16), pltpu.VMEM((spots, cells), BF16), pltpu.SemaphoreType.DMA((4,)),
        ],
        flops=4 * cells * spots * CAPACITY + 12 * cells * spots * width, name="first",
    )

    def products(first, parts, extra, size=None):
        count = sum(parts)
        return call(
            more_kernel, sc, (eth, etl, expression, extra),
            [whole((spots, cells)), whole((spots, cells)), genes_spec(first), whole((EXTRA, width))],
            tuple(sds((n, rows, width), F32) for n in parts), (ANY,) * len(parts), scratch=put_scratch,
            grid=(count,), flops=0 if size == 0 else 6 * cells * spots * width * count, name="more", size=size,
        )

    far_m, far1 = spot_move(compact, MIDDLE), spot_swap(compact, 1)
    top3, low3 = call(
        diagonal_kernel, sc, (b6, cell_swap(b7, 1)), [HBM] * 2,
        (sds((half, width), F32), sds((rows - half, width), F32)),
        (whole((half, width)), whole((rows - half, width))), name="diagonal", size=0,
        scratch=[pltpu.VMEM((rows, width), F32), pltpu.VMEM((rows, width), F32), pltpu.SemaphoreType.DMA((4,))],
    )
    in_top, in_low = cell_swap(top3, 2), cell_swap(low3, 4)
    (odd,) = products(2, (3,), tie(extra, top3), 0)
    far_n, far_e = spot_move(tie(far1, far_m, odd), MIDDLE), spot_move(tie(far_m, far1, odd), OUTWARD)
    in_odd = cell_swap(tie(odd, far1, far_m, in_top, in_low), 1)
    (even,) = products(5, (3,), tie(extra, odd, far1, far_m))
    one, two = call(
        merge_kernel, sc, (even, in_odd, in_low, in_top),
        [HBM] * 4, (block_sds, block_sds), (block_spec, block_spec), name="merge",
        scratch=[
            pltpu.VMEM((2, rows, width), F32), pltpu.VMEM((2, rows, width), F32), pltpu.VMEM((rows - half, width), F32),
            pltpu.VMEM((half, width), F32), pltpu.SemaphoreType.DMA((6,)),
        ],
    )
    in_x, in_y = cell_swap(one, 2), cell_swap(two, 4)
    far_f = spot_move(tie(far_n, far_e, one), OUTWARD)
    own_spatial = pl.BlockSpec((spots, width), lambda g, sc, *_: (0, sc[CELL]))
    small = whole((16, width))
    one_block = pl.BlockSpec((None, rows, width), lambda *_: (2, 0, 0))
    predicted, sums, extra_all, over = call(
        sums_kernel, sc, (even, in_odd, in_x, in_y, spatial),
        [one_block, one_block, block_spec, block_spec, own_spatial],
        (sds((spots, width), F32), sds((16, width), F32), sds((EXTRA, width), F32), sds((1,), F32)),
        (whole((spots, width)), small, whole((EXTRA, width)), SMEM), flops=5 * 10**9, name="sums",
    )
    all_sums = [sums, *(spot_swap(tie(sums, far_f), k) for k in range(1, n_spot))]
    maps_shape = (n_spot, CAPACITY, spots)
    comps = call(
        halves_kernel, sc, (tie(compact, sums), far1, far_n, far_e, far_m, far_f), [whole((CAPACITY, spots))] * 6,
        (sds(maps_shape, BF16),) * 2, (whole(maps_shape),) * 2, name="halves",
    )
    block, cosines = call(
        grad_kernel, sc, (tie(predicted, comps[0]), spatial, extra_all, *all_sums),
        [whole((spots, width)), own_spatial, whole((EXTRA, width))] + [small] * n_spot,
        (block_sds, sds((4, width), F32)), (block_spec, whole((4, width))), name="grad",
    )

    def pair(g, sc, qs):
        q = qs[0]
        for n, value in enumerate(qs):
            q = jnp.where(g == n, value, q) if n else q
        return (sc[CELL] // 2) ^ q

    def logit_part(got, qs, sums=None):
        blocks = [x for q in qs for x in got[q]]
        sizes = ((cells, spots), (EXTRA, width), (n_cell, EXTRA, 128))
        args = [expression, *blocks]
        specs = [
            pl.BlockSpec((cells, 2 * width), lambda g, sc, *_: (0, pair(g, sc, qs))), *[ANY] * len(blocks),
        ]
        outs, scratch = sizes, []
        if sums is not None:
            args += [hi, lo, *sums]
            specs += [whole((cells, spots)), whole((cells, spots)), *map(whole, sizes)]
            outs, scratch = ((cells, spots), (4,)), [pltpu.VMEM(size, F32) for size in sizes]
        steps = len(qs)
        return call(
            functools.partial(logit_kernel, steps, qs), sc, args, specs,
            tuple(sds(size, F32) for size in outs), tuple(whole(o) if len(o) > 1 else SMEM for o in outs), grid=(steps,),
            scratch=[*scratch, pltpu.VMEM((steps, 2, rows, width), F32), pltpu.SemaphoreType.DMA((steps, 2))],
            flops=12 * cells * spots * width * steps, name="logit",
        )

    def rows_part(gots, comps, qs, onto=None, space=ANY):
        blocks = [x for q in qs for got in gots for x in got[q]]
        args = [*blocks, *comps, place]
        specs = [space] * (len(blocks) + 2) + [whole((cells, 1))]
        alias = None
        if onto is not None:
            alias = {len(args) + 2: 0}
            args.append(onto)
            specs.append(ANY)
        steps = len(qs)
        return call(
            functools.partial(rows_kernel, steps, int(onto is not None)), (*sc, table), args, specs,
            sds((cells, genes), F32), pl.BlockSpec((cells, 2 * width), lambda g, sc, *_: (0, pair(g, sc, qs))),
            grid=(steps,), alias=alias,
            scratch=[
                pltpu.VMEM((steps, 8, rows, width), F32), pltpu.SemaphoreType.DMA((steps, 8)),
                pltpu.VMEM((4, CAPACITY, spots), BF16), pltpu.VMEM((4, CAPACITY, spots), BF16),
                pltpu.SemaphoreType.DMA((4, 2)),
                pltpu.VMEM((spots, 2 * width), BF16), pltpu.VMEM((spots, 2 * width), BF16),
                pltpu.VMEM((4, CAPACITY, 2 * width), F32),
                pltpu.VMEM((4 * WINDOW, 2 * width), BF16), pltpu.VMEM((4 * WINDOW, 2 * width), BF16),
            ],
            name="rows",
        )

    def expr_part(gots, maps, qs, near=None, final=False, onto=None):
        blocks = [x for q in qs for got in gots for x in got[q]]
        args = [*blocks, *(m for pairs in maps for m in pairs)]
        specs = [ANY] * len(blocks) + [whole((cells, spots))] * (2 * len(maps))
        columns = pl.BlockSpec((cells, 2 * width), lambda g, sc, *_: (0, pair(g, sc, qs)))
        steps_spec = pl.BlockSpec((None, cells, 2 * width), lambda g, sc, *_: (g, 0, 0))
        alias = None
        if near is not None:
            args.append(near)
            specs.append(steps_spec)
        if onto is not None:
            alias = {len(args) + 1: 0}
            args.append(onto)
            specs.append(ANY)
        out = sds((cells, genes) if final else (len(qs), cells, 2 * width), F32)
        scratch = [
            pltpu.VMEM((len(qs), 2 * len(maps), rows, width), F32),
            pltpu.SemaphoreType.DMA((len(qs), 2 * len(maps))),
        ]
        return call(
            functools.partial(expr_kernel, len(qs), len(maps), near is not None, onto is not None), sc, args, specs,
            out, columns if final else steps_spec, grid=(len(qs),), scratch=scratch, alias=alias,
            flops=6 * cells * spots * 2 * width * len(qs) * len(maps), name="expr",
        )

    def cores(x, *others):
        return (x, cell_swap(tie(x, *others) if others else x, 1))

    o_x, o_y = cell_swap(block, 2), cell_swap(block, 4)
    z1, mid = spot_swap(block, 1), spot_move(block, MIDDLE)
    got_o = {0: cores(block), 1: cores(o_x)}
    a_x, o_d = cell_swap(tie(z1, o_x), 2), cell_swap(tie(o_x, o_y, z1), 4)
    mid2, end2 = spot_move(tie(z1, mid), MIDDLE), spot_move(tie(mid, z1), OUTWARD)
    part = logit_part(got_o, (0, 1))
    z2 = tie(mid2, part[0]) + end2
    a_y = cell_swap(tie(z1, o_d, part[0]), 4)
    c_x = cell_swap(tie(z2, a_x, part[0]), 2)
    end3 = spot_move(tie(mid2, end2, part[0]), OUTWARD)
    got_o[2], got_o[3] = cores(o_y, part[0], a_x, z2), cores(o_d, part[0], a_x, z2)
    logit_grad, losses = logit_part(got_o, (2, 3), part)
    z3 = tie(mid, logit_grad) + end3
    c_y = cell_swap(tie(z2, a_y, logit_grad), 4)
    d_x = cell_swap(tie(z3, c_x, logit_grad), 2)
    early = (got_o[2][1], got_o[3][1])
    got_a, got_c = {0: cores(z1, *early)}, {0: cores(z2, *early)}
    got_d = {0: cores(z3, got_a[0][1], got_c[0][1], a_y, c_x)}
    gots = (got_o, got_a, got_c, got_d)
    body = rows_part(gots, comps, (0,))
    a_d, d_y = cell_swap(tie(a_y, d_x, body), 2), cell_swap(tie(z3, c_y, body), 4)
    early = (logit_grad, got_d[0][1])
    got_a[1], got_c[1] = cores(a_x, *early), cores(c_x, *early)
    got_d[1] = cores(d_x, got_a[1][1], got_c[1][1], body, c_y)
    body = rows_part(gots, comps, (1,), body)
    d_d, c_d = cell_swap(tie(d_y, a_d, body), 2), cell_swap(tie(c_x, d_y, body), 4)
    got_a[2], got_c[2] = cores(a_y, got_d[1][1]), cores(c_y, got_d[1][1])
    got_d[2] = cores(d_y, got_a[2][1], got_c[2][1], a_d, body)
    got_a[3] = cores(a_d, body, got_d[2][1])
    body = rows_part(gots, comps, (2,), body)
    got_c[3], got_d[3] = cores(c_d, body), cores(d_d, body)

    def direct(operands):
        body, last = operands[:2]
        return rows_part(last, comps, (3,), body, HBM)

    def exchange(operands):
        term = expr_part((operands[2],), ((hi, lo),), (0, 1, 2, 3), final=True)
        one, two, three = (spot_swap(term, k) for k in (1, 2, 3))
        return (term + one) + (two + three)

    expression_grad = lax.cond(
        over[0] > 0, exchange, direct, (body, [{3: got[3]} for got in gots], got_o)
    )

    return losses, predicted, cosines, logit_grad, expression_grad


def plain(logits, expression, spatial, spot_counts, cell_mask, cell_slide):
    spot_cols = logits.shape[1]
    gene_total = expression.shape[1]
    slide_total = spot_counts.shape[0]
    gene_rows = gene_total // lax.axis_size("cell")
    gene_start = lax.axis_index("cell") * gene_rows
    slide_ends = jnp.cumsum(spot_counts)
    spot_ids = lax.axis_index("spot") * spot_cols + jnp.arange(spot_cols, dtype=I32)
    spot_slide = jnp.sum((spot_ids[:, None] >= slide_ends[None, : slide_total - 1]).astype(I32), axis=1)
    member = (cell_mask[:, None] == 1) & (cell_slide[:, None] == spot_slide[None, :])
    onehot = (spot_slide[:, None] == jnp.arange(slide_total, dtype=I32)[None, :]).astype(F32)
    exponent = jnp.where(member, jnp.exp(logits), 0.0)
    column_total = lax.psum(jnp.sum(exponent, axis=0), "cell")
    mapping = exponent / column_total[None, :]
    predicted = lax.psum_scatter(
        lax.dot_general(expression, mapping, (((0,), (0,)), ((), ())), precision=HIGH),
        "cell", scatter_dimension=0, tiled=True,
    ).T
    spatial_own = lax.dynamic_slice_in_dim(spatial, gene_start, gene_rows, 1)
    sum_a, sum_b, sum_c = lax.psum(
        tuple(
            jnp.dot(onehot.T, t, precision=HIGH)
            for t in (predicted * spatial_own, predicted * predicted, spatial_own * spatial_own)
        ),
        "spot",
    )
    inverse_norms = lax.rsqrt(sum_b) * lax.rsqrt(sum_c)
    cosines = sum_a * inverse_norms
    spread_inv = jnp.dot(onehot, inverse_norms, precision=HIGH)
    spread_cos = jnp.dot(onehot, cosines / sum_b, precision=HIGH)
    pred_grad = -(spatial_own * spread_inv - predicted * spread_cos)
    losses, column_dot = lax.psum((-jnp.sum(cosines, axis=1), jnp.sum(predicted * pred_grad, axis=1)), "cell")
    grad_full = lax.all_gather(pred_grad, "cell", axis=1, tiled=True)
    map_grad = lax.dot_general(expression, grad_full, (((1,), (1,)), ((), ())), precision=HIGH)
    logit_grad = mapping * (map_grad - column_dot[None, :])
    expression_grad = lax.psum(jnp.dot(mapping, grad_full, precision=HIGH), "spot")
    return losses, predicted, cosines, logit_grad, expression_grad


def solution(mesh):
    small = mesh.shape["cell"] == 8 and mesh.shape["spot"] == 4
    return jax.shard_map(
        fast if small else plain,
        mesh=mesh,
        in_specs=(P("cell", "spot"), P("cell", None), P("spot", None), P(), P("cell"), P("cell")),
        out_specs=(P(), P("spot", "cell"), P(None, "cell"), P("cell", "spot"), P("cell", None)),
        check_vma=False,
    )
```

```python
import functools

import jax
import jax.numpy as jnp
from jax import lax
from jax.experimental import pallas as pl
from jax.experimental.pallas import tpu as pltpu
from jax.sharding import PartitionSpec as P

HIGH = lax.Precision.HIGHEST
F32, BF16, I32 = jnp.float32, jnp.bfloat16, jnp.int32
CAPACITY = 304
EXTRA = 8
WINDOW = 64
MIDDLE = ((1, 2), (2, 1))
OUTWARD = ((1, 0), (2, 3))
COUNTS, CELL, BASE, ORDER = 0, 4, 5, 9
BLOCKS = (7, 6, 3, 5, 1, 2, 4, 0)


def split(x):
    hi = x.astype(BF16)
    return hi, (x - hi.astype(F32)).astype(BF16)


def mm(a, b, dims=((1,), (0,))):
    return lax.dot_general(a, b, (dims, ((), ())), preferred_element_type=F32)


def mm3(ah, al, bh, bl, dims=((1,), (0,))):
    return mm(ah, bh, dims) + (mm(ah, bl, dims) + mm(al, bh, dims))


def slide_of(ids, sc):
    end, slide = 0, 0
    for k in range(3):
        end = end + sc[COUNTS + k]
        slide = slide + (ids >= end).astype(I32)
    return slide


def block_rows(t, step):
    return pl.ds(pl.multiple_of(t * step, step), step)


def first_kernel(sc, logits, mask, slide, expr, *refs):
    *kept, compact_out, extra_out, place_out, table_out = refs[:8]
    *outs, rbuf, obuf, sem, hi_out, lo_out, eth, etl, ksem = refs[8:]
    cells, spots = logits.shape
    cap, width = compact_out.shape[0], extra_out.shape[1]
    step = 128
    g = pl.program_id(0)

    @pl.when(g == 0)
    def _():
        lane = lax.broadcasted_iota(I32, (1, spots), 1) + sc[BASE]
        spot_slide = slide_of(lane, sc)
        lanes = lax.broadcasted_iota(I32, (1, step), 1).astype(F32)
        lower = (
            lax.broadcasted_iota(I32, (step, step), 0) > lax.broadcasted_iota(I32, (step, step), 1)
        ).astype(BF16)

        def body(t, carry):
            total, seen, widest = carry
            rows = block_rows(t, step)
            one = pl.ds(t, 1)
            own_row = jnp.where(mask[one, :] == 1, slide[one, :], -1).astype(F32)
            own = jnp.broadcast_to(own_row, (step, step)).T[:, :1]
            e = jnp.where(own.astype(I32) == spot_slide, jnp.exp(logits[rows, :]), 0.0)
            hi, lo = split(e)
            e = hi.astype(F32) + lo.astype(F32)
            hi, lo = split(e)
            hi_out[rows, :] = hi
            lo_out[rows, :] = lo
            hit, lit = split(e.T)
            eth[:, rows] = hit
            etl[:, rows] = lit
            onehot = (own == lanes).astype(F32)
            before = mm(lower, onehot.astype(BF16)) + seen
            rank = jnp.sum(onehot * before, axis=1, keepdims=True)
            rank = jnp.where(own >= 0, rank, -1.0)
            window = jnp.minimum((seen.astype(I32) // 8) * 8, cap - WINDOW)
            table_out[one, :] = window
            window = window.astype(F32)
            local = jnp.sum(onehot * (before - window), axis=1, keepdims=True) + WINDOW * own
            place_out[rows, :] = jnp.where(own >= 0, local, -1.0).astype(I32)
            row = jnp.broadcast_to(rank, (step, step)).T[:1, :].astype(I32)
            rbuf[:, rows] = (lax.broadcasted_iota(I32, (cap, step), 0) == row).astype(F32).astype(BF16)
            after = seen + jnp.sum(onehot, axis=0, keepdims=True)
            return total + jnp.sum(e, axis=0, keepdims=True), after, jnp.maximum(widest, after - window)

        zero = jnp.zeros((1, step), F32)
        total, seen, widest = lax.fori_loop(
            0, cells // step, body, (jnp.zeros((1, spots), F32), zero, zero), unroll=2
        )
        compact_out[...] = mm(rbuf[...], hi_out[...]) + mm(rbuf[...], lo_out[...])
        extra_out[...] = jnp.zeros_like(extra_out)
        for h in range(spots // width):
            extra_out[h : h + 1, :] = total[:, h * width : (h + 1) * width]
        over = jnp.maximum((seen > cap).astype(F32), (widest > WINDOW).astype(F32))
        over = jnp.max(over, axis=1, keepdims=True)
        extra_out[EXTRA - 1 : EXTRA, :] = jnp.broadcast_to(over, (1, width))
        load(list(zip((hi_out, lo_out, eth, etl), kept)), ksem)

    product(g, eth, etl, expr, extra_out, outs, obuf, sem)

    @pl.when(g == 1)
    def _():
        for n, (source, place) in enumerate(zip((hi_out, lo_out, eth, etl), kept)):
            pltpu.make_async_copy(source, place, ksem.at[n]).wait()


def product(g, eth, etl, expr, extra, outs, obuf, sem):
    spots = eth.shape[0]
    count = len(outs)
    slot = lax.rem(g, 2)

    def put(n):
        return pltpu.make_async_copy(obuf.at[n % 2], outs[n], sem.at[n % 2])

    for n in range(2, count):

        @pl.when(g == n)
        def _():
            put(n - 2).wait()

    xh, xl = split(expr[...])
    obuf[slot, :spots, :] = mm3(eth[...], etl[...], xh, xl)
    obuf[slot, spots:, :] = extra[...]
    for n in range(count):

        @pl.when(g == n)
        def _():
            put(n).start()

    @pl.when(g == count - 1)
    def _():
        for n in range(count - 2, count):
            put(n).wait()


def more_kernel(sc, eth, etl, expr, extra, *refs):
    *outs, obuf, sem = refs
    views = [out.at[n] for out in outs for n in range(out.shape[0])]
    product(pl.program_id(0), eth, etl, expr, extra, views, obuf, sem)


def load(pairs, sem):
    copies = [pltpu.make_async_copy(source, place, sem.at[n]) for n, (source, place) in enumerate(pairs)]
    for c in copies:
        c.start()
    return copies


def diagonal_kernel(sc, a, b, top, bottom, abuf, bbuf, sem):
    half = top.shape[0]
    upper, lower = pl.ds(0, half), pl.ds(half, bottom.shape[0])
    parts = [(x.at[r], y.at[r]) for r in (upper, lower) for x, y in ((a, abuf), (b, bbuf))]
    copies = load(parts, sem)
    for c in copies[:2]:
        c.wait()
    top[...] = abuf[upper, :] + bbuf[upper, :]
    for c in copies[2:]:
        c.wait()
    bottom[...] = abuf[lower, :] + bbuf[lower, :]


def merge_kernel(sc, a, b, low, high, one, two, abuf, bbuf, lbuf, hbuf, sem):
    half = high.shape[0]
    copies = load(
        [(a.at[0], abuf.at[0]), (b.at[0], bbuf.at[0]), (low, lbuf), (a.at[1], abuf.at[1]), (b.at[1], bbuf.at[1]), (high, hbuf)],
        sem,
    )
    for c in copies[:3]:
        c.wait()
    one[:half, :] = abuf[0, :half, :] + bbuf[0, :half, :]
    one[half:, :] = (abuf[0, half:, :] + bbuf[0, half:, :]) + lbuf[...]
    for c in copies[3:]:
        c.wait()
    two[:half, :] = (abuf[1, :half, :] + bbuf[1, :half, :]) + hbuf[...]
    two[half:, :] = abuf[1, half:, :] + bbuf[1, half:, :]


def totals(extra_rows, spots):
    width = extra_rows.shape[1]
    cols = [
        jnp.broadcast_to(extra_rows[h : h + 1, :], (128, width)).T[:, :1] for h in range(spots // width)
    ]
    return jnp.concatenate(cols, axis=0)


def sums_kernel(sc, a, b, x, y, spatial, pred_out, sums_out, extra_out, over_out):
    spots = pred_out.shape[0]
    extra = (a[spots:, :] + b[spots:, :]) + (x[spots:, :] + y[spots:, :])
    extra_out[...] = extra
    over_out[0] = extra[EXTRA - 1, 0]
    z = totals(extra, spots)
    pred = ((a[:spots, :] + b[:spots, :]) + (x[:spots, :] + y[:spots, :])) / z
    pred_out[...] = pred
    spat = spatial[...]
    ids = lax.broadcasted_iota(I32, (spots, 1), 0) + sc[BASE]
    slide = slide_of(ids, sc)
    sums_out[...] = jnp.zeros_like(sums_out)
    for n, term in enumerate((pred * spat, pred * pred, spat * spat)):
        for k in range(4):
            sums_out[4 * n + k : 4 * n + k + 1, :] = jnp.sum(
                jnp.where(slide == k, term, 0.0), axis=0, keepdims=True
            )


def grad_kernel(sc, pred, spatial, extra, s0, s1, s2, s3, blk_out, cos_out):
    spots, width = pred.shape
    sums = (s0[...] + s1[...]) + (s2[...] + s3[...])
    a, b, c = sums[0:4, :], sums[4:8, :], sums[8:12, :]
    inv = lax.rsqrt(b) * lax.rsqrt(c)
    cos = a * inv
    ratio = cos / b
    cos_out[...] = cos
    ids = lax.broadcasted_iota(I32, (spots, 1), 0) + sc[BASE]
    slide = slide_of(ids, sc)
    spread_inv, spread_cos = inv[3:4, :], ratio[3:4, :]
    for k in range(3):
        spread_inv = jnp.where(slide == k, inv[k : k + 1, :], spread_inv)
        spread_cos = jnp.where(slide == k, ratio[k : k + 1, :], spread_cos)
    p = pred[...]
    grad = -(spatial[...] * spread_inv - p * spread_cos) / totals(extra[...], spots)
    blk_out[:spots, :] = grad
    dots = lax.dot_general(
        jnp.ones((8, width), F32), p * grad, (((1,), (1,)), ((), ())),
        precision=HIGH, preferred_element_type=F32,
    )
    blk_out[spots:, :] = jnp.zeros((EXTRA, width), F32)
    for h in range(spots // width):
        blk_out[spots + h : spots + h + 1, :] = dots[:1, h * width : (h + 1) * width]
    blk_out[spots + 4 : spots + 8, :] = cos


def fetch(g, steps, blocks, buf, sem):
    per = len(blocks) // steps

    def copies(s):
        return [pltpu.make_async_copy(blocks[s * per + n], buf.at[s, n], sem.at[s, n]) for n in range(per)]

    @pl.when(g == 0)
    def _():
        for s in range(steps):
            for c in copies(s):
                c.start()

    for s in range(steps):

        @pl.when(g == s)
        def _():
            for c in copies(s):
                c.wait()

    return buf.at[g]


def logit_kernel(steps, qs, sc, expr, *refs):
    blocks, refs = refs[: 2 * steps], refs[2 * steps :]
    final = qs[0] > 0
    if final:
        hi, lo, acc_in, dots_in, parts_in, out, loss_out, acc, dots, parts, buf, sem = refs
    else:
        acc, dots, parts, buf, sem = refs
    g = pl.program_id(0)
    cells, spots = acc.shape
    width = buf.shape[3]
    got = fetch(g, steps, blocks, buf, sem)

    @pl.when(g == 0)
    def _():
        dots[...] = dots_in[...] if final else jnp.zeros_like(dots)
        if final:
            parts[...] = parts_in[...]
        else:
            parts[...] = jnp.zeros_like(parts)

    parity = lax.rem(sc[CELL], 2)

    def add(first):
        halves = []
        for side in range(2):
            start = pl.multiple_of(jnp.where(parity == side, 0, width), width)
            gh, gl = split(got[side, :spots, :])
            dots[...] += got[side, spots:, :]
            sums = jnp.sum(got[side, spots:, :], axis=1, keepdims=True)
            parts[sc[CELL] ^ (2 * (g + qs[0]) + side)] = jnp.broadcast_to(sums, parts.shape[1:])
            halves.append((start, gh, gl))

        def body(t, _):
            rows = block_rows(t, 512)
            value = None
            for start, gh, gl in halves:
                xh, xl = split(expr[rows, pl.ds(start, width)])
                term = mm3(xh, xl, gh, gl, ((1,), (1,)))
                value = term if value is None else value + term
            if not first:
                acc[rows, :] += value
            elif final:
                acc[rows, :] = acc_in[rows, :] + value
            else:
                acc[rows, :] = value
            return 0

        lax.fori_loop(0, cells // 512, body, 0, unroll=True)

    @pl.when(g == 0)
    def _():
        add(True)

    @pl.when(g > 0)
    def _():
        add(False)

    if final:

        @pl.when(g == steps - 1)
        def _():
            row = jnp.concatenate([dots[h : h + 1, :] for h in range(spots // width)], axis=1)
            e = hi[...].astype(F32) + lo[...].astype(F32)
            out[...] = e * (acc[...] - row)
            total = parts[0]
            for n in range(1, parts.shape[0]):
                total = total + parts[n]
            for k in range(4):
                loss_out[k] = -total[4 + k, 0]


def halves_kernel(sc, compact, far1, far_n, far_e, far_m, far_f, hi_out, lo_out):
    spots = compact.shape[1]
    middle = (sc[BASE] == spots) | (sc[BASE] == 2 * spots)
    two = jnp.where(middle, far_n[...], far_e[...])
    three = jnp.where(middle, far_m[...], far_f[...])
    for n, value in enumerate((compact[...], far1[...], two, three)):
        hi_out[n], lo_out[n] = split(value)


def rows_kernel(steps, alias, sc, table, *refs):
    blocks, refs = refs[: 8 * steps], refs[8 * steps :]
    (maps_hi, maps_lo, place), refs = refs[:3], refs[3 + alias :]
    out, buf, sem, mh, ml, msem, gh, gl, res, sh, sl = refs
    g = pl.program_id(0)
    cells = out.shape[0]
    cap, spots = mh.shape[1:]
    width = buf.shape[3]
    half = spots // 2

    def bring(s, n):
        return pltpu.make_async_copy(blocks[8 * s + n], buf.at[s, n], sem.at[s, n])

    def bring_maps(n):
        return [
            pltpu.make_async_copy(maps_hi.at[n], mh.at[n], msem.at[n, 0]),
            pltpu.make_async_copy(maps_lo.at[n], ml.at[n], msem.at[n, 1]),
        ]

    own = sc[BASE] // spots

    @pl.when(g == 0)
    def _():
        for s in range(steps):
            for n in range(4):
                if s == 0:
                    for c in bring_maps(n):
                        c.start()
                for side in range(2):
                    bring(s, 2 * n + side).start()

    parity = lax.rem(sc[CELL], 2)

    def layer_body(layer, _):
        partner = layer ^ own
        for side in range(2):
            n = 2 * partner + side
            pltpu.make_async_copy(blocks[0], buf.at[g, n], sem.at[g, n]).wait()

        @pl.when(g == 0)
        def _():
            for c in bring_maps(partner):
                c.wait()

        for side in range(2):
            start = pl.multiple_of(jnp.where(parity == side, 0, width), width)
            hi, lo = split(buf[g, 2 * partner + side, :spots, :])
            gh[:, pl.ds(start, width)] = hi
            gl[:, pl.ds(start, width)] = lo
        base = layer * spots
        low, low_end = slide_of(base, sc), slide_of(base + half - 1, sc)
        high, high_end = slide_of(base + half, sc), slide_of(base + spots - 1, sc)
        before = jnp.where(layer == 0, -1, slide_of(base - 1, sc))

        def put(k, value):
            res[k] = jnp.where(k > before, 0.0, res[k]) + value

        @pl.when(low == high_end)
        def _():
            put(low, mm3(mh[partner], ml[partner], gh[...], gl[...]))

        def slide_body(k, _):
            in_low, in_high = k <= low_end, k >= high

            def part(first, count):
                cols = pl.ds(first, count)
                ids = lax.broadcasted_iota(I32, (1, count), 1) + (base + first)
                keep = (slide_of(ids, sc) == k).astype(F32).astype(BF16)
                put(k, mm3(mh[partner, :, cols] * keep, ml[partner, :, cols] * keep, gh[cols, :], gl[cols, :]))

            @pl.when(in_low & in_high)
            def _():
                part(0, spots)

            @pl.when(jnp.logical_not(in_low & in_high))
            def _():
                part(pl.multiple_of(jnp.where(in_low, 0, half), half), half)

            return 0

        lax.fori_loop(low, jnp.where(low == high_end, low, high_end + 1), slide_body, 0)
        return 0

    lax.fori_loop(0, 4, layer_body, 0)
    slots = lax.broadcasted_iota(I32, (1, 4 * WINDOW), 1)

    def place_body(t, _):
        rows = block_rows(t, 128)
        for k in range(4):
            window = pl.ds(pl.multiple_of(table[t, k], 8), WINDOW)
            hi, lo = split(res[k, window, :])
            sh[k * WINDOW : (k + 1) * WINDOW, :] = hi
            sl[k * WINDOW : (k + 1) * WINDOW, :] = lo
        pick = (place[rows, :] == slots).astype(F32).astype(BF16)
        out[rows, :] = mm(pick, sh[...]) + mm(pick, sl[...])
        return 0

    lax.fori_loop(0, cells // 128, place_body, 0, unroll=8)


def expr_kernel(steps, layers, near, alias, sc, *refs):
    refs = list(refs)
    blocks = [refs.pop(0) for _ in range(2 * layers * steps)]
    maps = [(refs.pop(0), refs.pop(0)) for _ in range(layers)]
    acc = refs.pop(0) if near else None
    if alias:
        refs.pop(0)
    out, buf, sem = refs
    g = pl.program_id(0)
    cells, spots = maps[0][0].shape
    width = buf.shape[3]
    got = fetch(g, steps, blocks, buf, sem)
    parity = lax.rem(sc[CELL], 2)
    for side in range(2):
        start = pl.multiple_of(jnp.where(parity == side, 0, width), width)
        grads = [split(got[2 * n + side, :spots, :]) for n in range(layers)]

        def body(t, _):
            rows = block_rows(t, 256)
            value = None
            for (mh, ml), (gh, gl) in zip(maps, grads):
                term = mm3(mh[rows, :], ml[rows, :], gh, gl)
                value = term if value is None else value + term
            if acc is not None:
                value = acc[rows, pl.ds(start, width)] + value
            out[rows, pl.ds(start, width)] = value
            return 0

        lax.fori_loop(0, cells // 256, body, 0, unroll=True)


def tie(x, *others):
    return lax.optimization_barrier((x, *others))[0]


def whole(shape):
    return pl.BlockSpec(shape, lambda *_: (0,) * len(shape))


ANY = pl.BlockSpec(memory_space=pl.ANY)
HBM = pl.BlockSpec(memory_space=pltpu.HBM)
SMEM = pl.BlockSpec(memory_space=pltpu.SMEM)


def call(kernel, sc, args, in_specs, outs, out_specs, grid=(1,), scratch=(), flops=0, name=None, alias=None, size=None):
    if size is None:
        size = sum(x.size * x.dtype.itemsize for x in (*args, *jax.tree.leaves(outs)))
    return pl.pallas_call(
        kernel,
        out_shape=outs,
        grid_spec=pltpu.PrefetchScalarGridSpec(
            num_scalar_prefetch=len(sc), grid=grid, in_specs=in_specs, out_specs=out_specs, scratch_shapes=scratch
        ),
        cost_estimate=pl.CostEstimate(flops=flops, bytes_accessed=size, transcendentals=0),
        input_output_aliases=alias or {},
        name=name,
    )(*sc, *args)


def fast(logits, expression, spatial, spot_counts, cell_mask, cell_slide):
    cells, spots = logits.shape
    genes = expression.shape[1]
    n_cell, n_spot = lax.axis_size("cell"), lax.axis_size("spot")
    width = genes // n_cell
    half, rows = spots // 2, spots + EXTRA
    ci, zi = lax.axis_index("cell"), lax.axis_index("spot")
    places = [ci, *((zi ^ k) * spots for k in range(n_spot))]
    sc = (jnp.concatenate([spot_counts, jnp.stack(places), jnp.array(BLOCKS, I32)]).astype(I32),)
    sds = jax.ShapeDtypeStruct
    block_sds, block_spec = sds((rows, width), F32), whole((rows, width))

    put_scratch = [pltpu.VMEM((2, rows, width), F32), pltpu.SemaphoreType.DMA((2,))]

    def cell_swap(x, bit):
        return lax.ppermute(x, "cell", [(i, i ^ bit) for i in range(n_cell)])

    def spot_swap(x, k):
        return lax.ppermute(x, "spot", [(i, i ^ k) for i in range(n_spot)])

    def spot_move(x, moves):
        return lax.ppermute(x, "spot", moves)

    def genes_spec(first):
        return pl.BlockSpec((cells, width), lambda g, sc, *_: (0, sc[CELL] ^ sc[ORDER + first + g]))

    hi, lo, eth, etl, compact, extra, place, table, b7, b6 = call(
        first_kernel, sc, (logits, cell_mask.reshape(-1, 128), cell_slide.reshape(-1, 128), expression),
        [whole((cells, spots)), whole((cells // 128, 128)), whole((cells // 128, 128)), genes_spec(0)],
        (
            sds((cells, spots), BF16), sds((cells, spots), BF16), sds((spots, cells), BF16), sds((spots, cells), BF16),
            sds((CAPACITY, spots), F32), sds((EXTRA, width), F32), sds((cells, 1), I32), sds((cells // 128, 128), I32),
            block_sds, block_sds,
        ),
        (
            HBM, HBM, HBM, HBM, whole((CAPACITY, spots)), whole((EXTRA, width)), whole((cells, 1)), whole((cells // 128, 128)), ANY, ANY,
        ),
        grid=(2,), scratch=[
            pltpu.VMEM((CAPACITY, cells), BF16), *put_scratch, pltpu.VMEM((cells, spots), BF16), pltpu.VMEM((cells, spots), BF16),
            pltpu.VMEM((spots, cells), BF16), pltpu.VMEM((spots, cells), BF16), pltpu.SemaphoreType.DMA((4,)),
        ],
        flops=4 * cells * spots * CAPACITY + 12 * cells * spots * width, name="first",
    )

    def products(first, parts, extra, size=None):
        count = sum(parts)
        return call(
            more_kernel, sc, (eth, etl, expression, extra),
            [whole((spots, cells)), whole((spots, cells)), genes_spec(first), whole((EXTRA, width))],
            tuple(sds((n, rows, width), F32) for n in parts), (ANY,) * len(parts), scratch=put_scratch,
            grid=(count,), flops=0 if size == 0 else 6 * cells * spots * width * count, name="more", size=size,
        )

    far_m, far1 = spot_move(compact, MIDDLE), spot_swap(compact, 1)
    top3, low3 = call(
        diagonal_kernel, sc, (b6, cell_swap(b7, 1)), [HBM] * 2,
        (sds((half, width), F32), sds((rows - half, width), F32)),
        (whole((half, width)), whole((rows - half, width))), name="diagonal", size=0,
        scratch=[pltpu.VMEM((rows, width), F32), pltpu.VMEM((rows, width), F32), pltpu.SemaphoreType.DMA((4,))],
    )
    in_top, in_low = cell_swap(top3, 2), cell_swap(low3, 4)
    (odd,) = products(2, (3,), tie(extra, top3), 0)
    far_n, far_e = spot_move(tie(far1, far_m, odd), MIDDLE), spot_move(tie(far_m, far1, odd), OUTWARD)
    in_odd = cell_swap(tie(odd, far1, far_m, in_top, in_low), 1)
    (even,) = products(5, (3,), tie(extra, odd, far1, far_m))
    one, two = call(
        merge_kernel, sc, (even, in_odd, in_low, in_top),
        [HBM] * 4, (block_sds, block_sds), (block_spec, block_spec), name="merge",
        scratch=[
            pltpu.VMEM((2, rows, width), F32), pltpu.VMEM((2, rows, width), F32), pltpu.VMEM((rows - half, width), F32),
            pltpu.VMEM((half, width), F32), pltpu.SemaphoreType.DMA((6,)),
        ],
    )
    in_x, in_y = cell_swap(one, 2), cell_swap(two, 4)
    far_f = spot_move(tie(far_n, far_e, one), OUTWARD)
    own_spatial = pl.BlockSpec((spots, width), lambda g, sc, *_: (0, sc[CELL]))
    small = whole((16, width))
    one_block = pl.BlockSpec((None, rows, width), lambda *_: (2, 0, 0))
    predicted, sums, extra_all, over = call(
        sums_kernel, sc, (even, in_odd, in_x, in_y, spatial),
        [one_block, one_block, block_spec, block_spec, own_spatial],
        (sds((spots, width), F32), sds((16, width), F32), sds((EXTRA, width), F32), sds((1,), F32)),
        (whole((spots, width)), small, whole((EXTRA, width)), SMEM), flops=5 * 10**9, name="sums",
    )
    all_sums = [sums, *(spot_swap(tie(sums, far_f), k) for k in range(1, n_spot))]
    maps_shape = (n_spot, CAPACITY, spots)
    comps = call(
        halves_kernel, sc, (tie(compact, sums), far1, far_n, far_e, far_m, far_f), [whole((CAPACITY, spots))] * 6,
        (sds(maps_shape, BF16),) * 2, (whole(maps_shape),) * 2, name="halves",
    )
    block, cosines = call(
        grad_kernel, sc, (tie(predicted, comps[0]), spatial, extra_all, *all_sums),
        [whole((spots, width)), own_spatial, whole((EXTRA, width))] + [small] * n_spot,
        (block_sds, sds((4, width), F32)), (block_spec, whole((4, width))), name="grad",
    )

    def pair(g, sc, qs):
        q = qs[0]
        for n, value in enumerate(qs):
            q = jnp.where(g == n, value, q) if n else q
        return (sc[CELL] // 2) ^ q

    def logit_part(got, qs, sums=None):
        blocks = [x for q in qs for x in got[q]]
        sizes = ((cells, spots), (EXTRA, width), (n_cell, EXTRA, 128))
        args = [expression, *blocks]
        specs = [
            pl.BlockSpec((cells, 2 * width), lambda g, sc, *_: (0, pair(g, sc, qs))), *[ANY] * len(blocks),
        ]
        outs, scratch = sizes, []
        if sums is not None:
            args += [hi, lo, *sums]
            specs += [whole((cells, spots)), whole((cells, spots)), *map(whole, sizes)]
            outs, scratch = ((cells, spots), (4,)), [pltpu.VMEM(size, F32) for size in sizes]
        steps = len(qs)
        return call(
            functools.partial(logit_kernel, steps, qs), sc, args, specs,
            tuple(sds(size, F32) for size in outs), tuple(whole(o) if len(o) > 1 else SMEM for o in outs), grid=(steps,),
            scratch=[*scratch, pltpu.VMEM((steps, 2, rows, width), F32), pltpu.SemaphoreType.DMA((steps, 2))],
            flops=12 * cells * spots * width * steps, name="logit",
        )

    def rows_part(gots, comps, qs, onto=None, space=ANY):
        blocks = [x for q in qs for got in gots for x in got[q]]
        args = [*blocks, *comps, place]
        specs = [space] * (len(blocks) + 2) + [whole((cells, 1))]
        alias = None
        if onto is not None:
            alias = {len(args) + 2: 0}
            args.append(onto)
            specs.append(ANY)
        steps = len(qs)
        return call(
            functools.partial(rows_kernel, steps, int(onto is not None)), (*sc, table), args, specs,
            sds((cells, genes), F32), pl.BlockSpec((cells, 2 * width), lambda g, sc, *_: (0, pair(g, sc, qs))),
            grid=(steps,), alias=alias,
            scratch=[
                pltpu.VMEM((steps, 8, rows, width), F32), pltpu.SemaphoreType.DMA((steps, 8)),
                pltpu.VMEM((4, CAPACITY, spots), BF16), pltpu.VMEM((4, CAPACITY, spots), BF16),
                pltpu.SemaphoreType.DMA((4, 2)),
                pltpu.VMEM((spots, 2 * width), BF16), pltpu.VMEM((spots, 2 * width), BF16),
                pltpu.VMEM((4, CAPACITY, 2 * width), F32),
                pltpu.VMEM((4 * WINDOW, 2 * width), BF16), pltpu.VMEM((4 * WINDOW, 2 * width), BF16),
            ],
            name="rows",
        )

    def expr_part(gots, maps, qs, near=None, final=False, onto=None):
        blocks = [x for q in qs for got in gots for x in got[q]]
        args = [*blocks, *(m for pairs in maps for m in pairs)]
        specs = [ANY] * len(blocks) + [whole((cells, spots))] * (2 * len(maps))
        columns = pl.BlockSpec((cells, 2 * width), lambda g, sc, *_: (0, pair(g, sc, qs)))
        steps_spec = pl.BlockSpec((None, cells, 2 * width), lambda g, sc, *_: (g, 0, 0))
        alias = None
        if near is not None:
            args.append(near)
            specs.append(steps_spec)
        if onto is not None:
            alias = {len(args) + 1: 0}
            args.append(onto)
            specs.append(ANY)
        out = sds((cells, genes) if final else (len(qs), cells, 2 * width), F32)
        scratch = [
            pltpu.VMEM((len(qs), 2 * len(maps), rows, width), F32),
            pltpu.SemaphoreType.DMA((len(qs), 2 * len(maps))),
        ]
        return call(
            functools.partial(expr_kernel, len(qs), len(maps), near is not None, onto is not None), sc, args, specs,
            out, columns if final else steps_spec, grid=(len(qs),), scratch=scratch, alias=alias,
            flops=6 * cells * spots * 2 * width * len(qs) * len(maps), name="expr",
        )

    def cores(x, *others):
        return (x, cell_swap(tie(x, *others) if others else x, 1))

    o_x, o_y = cell_swap(block, 2), cell_swap(block, 4)
    z1, mid = spot_swap(block, 1), spot_move(block, MIDDLE)
    got_o = {0: cores(block), 1: cores(o_x)}
    a_x, o_d = cell_swap(tie(z1, o_x), 2), cell_swap(tie(o_x, o_y, z1), 4)
    mid2, end2 = spot_move(tie(z1, mid), MIDDLE), spot_move(tie(mid, z1), OUTWARD)
    part = logit_part(got_o, (0, 1))
    z2 = tie(mid2, part[0]) + end2
    a_y = cell_swap(tie(z1, o_d, part[0]), 4)
    c_x = cell_swap(tie(z2, a_x, part[0]), 2)
    end3 = spot_move(tie(mid2, end2, part[0]), OUTWARD)
    got_o[2], got_o[3] = cores(o_y, part[0], a_x, z2), cores(o_d, part[0], a_x, z2)
    logit_grad, losses = logit_part(got_o, (2, 3), part)
    z3 = tie(mid, logit_grad) + end3
    c_y = cell_swap(tie(z2, a_y, logit_grad), 4)
    d_x = cell_swap(tie(z3, c_x, logit_grad), 2)
    early = (got_o[2][1], got_o[3][1])
    got_a, got_c = {0: cores(z1, *early)}, {0: cores(z2, *early)}
    got_d = {0: cores(z3, got_a[0][1], got_c[0][1], a_y, c_x)}
    gots = (got_o, got_a, got_c, got_d)
    body = rows_part(gots, comps, (0,))
    a_d, d_y = cell_swap(tie(a_y, d_x, body), 2), cell_swap(tie(z3, c_y, body), 4)
    early = (logit_grad, got_d[0][1])
    got_a[1], got_c[1] = cores(a_x, *early), cores(c_x, *early)
    got_d[1] = cores(d_x, got_a[1][1], got_c[1][1], body, c_y)
    body = rows_part(gots, comps, (1,), body)
    d_d, c_d = cell_swap(tie(d_y, a_d, body), 2), cell_swap(tie(c_x, d_y, body), 4)
    got_a[2], got_c[2] = cores(a_y, got_d[1][1]), cores(c_y, got_d[1][1])
    got_d[2] = cores(d_y, got_a[2][1], got_c[2][1], a_d, body)
    got_a[3] = cores(a_d, body, got_d[2][1])
    body = rows_part(gots, comps, (2,), body)
    got_c[3], got_d[3] = cores(c_d, body), cores(d_d, body)

    def direct(operands):
        body, last = operands[:2]
        return rows_part(last, comps, (3,), body, HBM)

    def exchange(operands):
        term = expr_part((operands[2],), ((hi, lo),), (0, 1, 2, 3), final=True)
        one, two, three = (spot_swap(term, k) for k in (1, 2, 3))
        return (term + one) + (two + three)

    expression_grad = lax.cond(
        over[0] > 0, exchange, direct, (body, [{3: got[3]} for got in gots], got_o)
    )

    return losses, predicted, cosines, logit_grad, expression_grad


def plain(logits, expression, spatial, spot_counts, cell_mask, cell_slide):
    spot_cols = logits.shape[1]
    gene_total = expression.shape[1]
    slide_total = spot_counts.shape[0]
    gene_rows = gene_total // lax.axis_size("cell")
    gene_start = lax.axis_index("cell") * gene_rows
    slide_ends = jnp.cumsum(spot_counts)
    spot_ids = lax.axis_index("spot") * spot_cols + jnp.arange(spot_cols, dtype=I32)
    spot_slide = jnp.sum((spot_ids[:, None] >= slide_ends[None, : slide_total - 1]).astype(I32), axis=1)
    member = (cell_mask[:, None] == 1) & (cell_slide[:, None] == spot_slide[None, :])
    onehot = (spot_slide[:, None] == jnp.arange(slide_total, dtype=I32)[None, :]).astype(F32)
    exponent = jnp.where(member, jnp.exp(logits), 0.0)
    column_total = lax.psum(jnp.sum(exponent, axis=0), "cell")
    mapping = exponent / column_total[None, :]
    predicted = lax.psum_scatter(
        lax.dot_general(expression, mapping, (((0,), (0,)), ((), ())), precision=HIGH),
        "cell", scatter_dimension=0, tiled=True,
    ).T
    spatial_own = lax.dynamic_slice_in_dim(spatial, gene_start, gene_rows, 1)
    sum_a, sum_b, sum_c = lax.psum(
        tuple(
            jnp.dot(onehot.T, t, precision=HIGH)
            for t in (predicted * spatial_own, predicted * predicted, spatial_own * spatial_own)
        ),
        "spot",
    )
    inverse_norms = lax.rsqrt(sum_b) * lax.rsqrt(sum_c)
    cosines = sum_a * inverse_norms
    spread_inv = jnp.dot(onehot, inverse_norms, precision=HIGH)
    spread_cos = jnp.dot(onehot, cosines / sum_b, precision=HIGH)
    pred_grad = -(spatial_own * spread_inv - predicted * spread_cos)
    losses, column_dot = lax.psum((-jnp.sum(cosines, axis=1), jnp.sum(predicted * pred_grad, axis=1)), "cell")
    grad_full = lax.all_gather(pred_grad, "cell", axis=1, tiled=True)
    map_grad = lax.dot_general(expression, grad_full, (((1,), (1,)), ((), ())), precision=HIGH)
    logit_grad = mapping * (map_grad - column_dot[None, :])
    expression_grad = lax.psum(jnp.dot(mapping, grad_full, precision=HIGH), "spot")
    return losses, predicted, cosines, logit_grad, expression_grad


def solution(mesh):
    small = mesh.shape["cell"] == 8 and mesh.shape["spot"] == 4
    return jax.shard_map(
        fast if small else plain,
        mesh=mesh,
        in_specs=(P("cell", "spot"), P("cell", None), P("spot", None), P(), P("cell"), P("cell")),
        out_specs=(P(), P("spot", "cell"), P(None, "cell"), P("cell", "spot"), P("cell", None)),
        check_vma=False,
    )
```
